512 devices in a mesh: mem: 32 (over z, y_hi, core), gy: 4 (over y_lo), gx: 4 (over x).
Axes of the slice: x: 4, y: 8 (y_hi: 2, y_lo: 4; y = y_hi * 4 + y_lo), z: 8, core: 2. Of those that a mesh axis runs over, the one named last changes fastest.
Arguments:
- increment: float32 [4, 256, 4096], P(None, 'gy', 'gx'), may hold values from -6 to 6
- members: float32 [32, 4, 256, 4096], P('mem', None, 'gy', 'gx'), may hold values from -6 to 6
- zonal_diff: float32 [256, 4096], P('gy', 'gx'), may hold values from 0.05 to 0.35
- merid_diff: float32 [256, 4096], P('gy', 'gx'), may hold values from 0.02 to 0.15
- sea_mask: int32 [256, 4096], P('gy', 'gx'), may hold values 0 or 1
Outputs:
- product: float32 [4, 256, 4096], P(None, 'gy', 'gx')
The draws below stay inside these ranges and needn't reach their ends.
All inputs are finite; a program needn't handle non-finite values. No bound on the sum of `sea_mask` on one device may be relied on, other than what follows from the above.
Results may differ from the reference program's by a relative error of at most 0.00002.
Values sent between devices are 32-bit elements; how exact they have to be, the bound alone decides.
A program may use at most 64 MiB of HBM per device.

```python
import math
import jax
import jax.numpy as jnp
from jax import lax

LEVELS = 4
STEPS = 4
MEMBERS = 32
NX = 4096
NY = 256


def place_ends(entries, rng, smallest, top_value):
    extent = entries.shape
    place = [jax.random.randint(jax.random.fold_in(rng, axis), (), 0, extent[axis]) for axis in range(len(extent))]
    entries = entries.at[tuple(place)].set(smallest)
    longest = extent.index(max(extent))
    place[longest] = (place[longest] + 1) % extent[longest]
    return entries.at[tuple(place)].set(top_value)


def levels(stream_key, extent, pieces, low, high):
    def one(axis_at, parts):
        steps = jax.random.uniform(jax.random.fold_in(jax.random.fold_in(stream_key, 6), axis_at), (parts,), jnp.float32, low / len(pieces), high / len(pieces))
        return jnp.repeat(jnp.exp(steps), extent[axis_at] // parts).reshape((-1,) + (1,) * (len(extent) - axis_at - 1))

    level = one(*pieces[0])
    for cut in pieces[1:]:
        level = level * one(*cut)
    return level


def noise(stream_key, dims, deviation, reach, split=(), dtype=jnp.bfloat16):
    level = levels(stream_key, dims, split, -0.22, 0.18) if split else 1.0
    drawn = jax.random.normal(stream_key, dims, jnp.float32) * deviation * level
    return jnp.minimum(jnp.maximum(drawn, -reach), reach).astype(dtype)


def setup_inputs(seed: int = 0) -> dict:
    seeds = jax.random.split(jax.random.key(seed), 6)
    increment = noise(seeds[0], (LEVELS, NY, NX), 1.0, 6.0, ((1, 4), (2, 4)), jnp.float32)
    members = noise(seeds[1], (MEMBERS, LEVELS, NY, NX), 1.0, 6.0, ((0, 32), (2, 4), (3, 4)), jnp.float32)
    zonal_diff = jnp.clip(jnp.exp(math.log(0.35) - 1.9459101 * jax.random.uniform(seeds[2], (NY, NX), jnp.float32) ** levels(seeds[2], (NY, NX), ((0, 4), (1, 4)), -0.2, 0.2)), 0.05, 0.35)
    merid_diff = jnp.clip(jnp.exp(math.log(0.15) - 2.014903 * jax.random.uniform(seeds[3], (NY, NX), jnp.float32) ** levels(seeds[3], (NY, NX), ((0, 4), (1, 4)), -0.2, 0.2)), 0.02, 0.15)
    sea_mask = place_ends((jax.random.randint(seeds[4], (NY, NX), 0, 8) < 7).astype(jnp.int32), jax.random.fold_in(seeds[4], 1), 0, 1)
    return dict(increment=increment, members=members, zonal_diff=zonal_diff, merid_diff=merid_diff, sea_mask=sea_mask)


def widen(field):
    field = jnp.concatenate([field[..., -1:], field, field[..., :1]], axis=-1)
    zero_row = jnp.zeros(field.shape[:-2] + (1, field.shape[-1]), jnp.float32)
    return jnp.concatenate([zero_row, field, zero_row], axis=-2)


def face_weights(zonal, merid, wet):
    east = zonal[:, :-1] * wet[:, :-1] * wet[:, 1:]
    north = merid[:-1, :] * wet[:-1, :] * wet[1:, :]
    return east, north


def sweep(field, east, north):
    centre = field[:, 1:-1, 1:-1]
    go_east = east[1:-1, 1:] * (field[:, 1:-1, 2:] - centre)
    go_west = east[1:-1, :-1] * (centre - field[:, 1:-1, :-2])
    go_north = north[1:, 1:-1] * (field[:, 2:, 1:-1] - centre)
    go_south = north[:-1, 1:-1] * (centre - field[:, :-2, 1:-1])
    return centre + go_east - go_west + go_north - go_south


def reference(increment, members, zonal_diff, merid_diff, sea_mask):
    wet = sea_mask.astype(jnp.float32)
    east, north = face_weights(widen(zonal_diff), widen(merid_diff), widen(wet))

    def one_member(total, member):
        field = member * increment * wet
        for step in range(STEPS):
            field = sweep(widen(field), east, north)
        return total + member * field, None

    total, unused = lax.scan(one_member, jnp.zeros(increment.shape, jnp.float32), members)
    return total
```

```python
import jax
import jax.numpy as jnp
from jax import lax
from jax.experimental import pallas as pl
from jax.experimental.pallas import tpu as pltpu
from jax.sharding import PartitionSpec as P

STEPS = 4
LEVELS = 4
ROWS = 64
COLS = 1024
XROWS = ROWS + 8
XCOLS = COLS + 128
HALF = COLS // 2
MESH = pl.DeviceIdType.MESH
F32 = jnp.float32


def kernel(
    inc_hbm, mem_hbm, zon_hbm, mer_hbm, sea_hbm, out,
    inc, mem, zon, mer, sea,
    field, other, wet, east, north,
    rows_out, rows_in, cols_out, cols_in, corner_in,
    term, peer, part, gathered, mine, across,
    load_sem, halo_send, halo_recv, core_send, core_recv,
    red_send, red_recv, y_send, y_recv, ag_send, ag_recv, fwd_send, fwd_recv,
):
    me = lax.axis_index("mem")
    gy = lax.axis_index("gy")
    gx = lax.axis_index("gx")
    z = me // 4
    hi = lax.rem(me // 2, 2)
    core = lax.rem(me, 2)

    def member_at(z_, hi_, core_):
        return z_ * 4 + hi_ * 2 + core_

    def beside(dy, dx):
        y = lax.rem(hi * 4 + gy + dy + 8, 8)
        return (member_at(z, y // 4, core), lax.rem(y, 4), lax.rem(gx + dx + 4, 4))

    def along(k):
        return (member_at(lax.rem(z + k, 8), hi, core), gy, gx)

    core_peer = (member_at(z, hi, 1 - core), gy, gx)
    y_peer = (member_at(z, 1 - hi, core), gy, gx)

    barrier = pltpu.get_barrier_semaphore()
    around = [(-1, 0), (1, 0), (0, -1), (0, 1), (-1, -1), (1, -1), (-1, 1), (1, 1)]
    partners = [beside(dy, dx) for dy, dx in around]
    partners += [core_peer, y_peer] + [along(k) for k in range(1, 8)]
    for device in partners:
        pl.semaphore_signal(barrier, inc=1, device_id=device, device_id_type=MESH)

    loads = [
        pltpu.make_async_copy(sea_hbm, sea, load_sem.at[0]),
        pltpu.make_async_copy(zon_hbm, zon, load_sem.at[1]),
        pltpu.make_async_copy(mer_hbm, mer, load_sem.at[2]),
        pltpu.make_async_copy(inc_hbm, inc, load_sem.at[3]),
        pltpu.make_async_copy(mem_hbm.at[0], mem, load_sem.at[4]),
    ]
    for load in loads:
        load.start()
    for load in loads:
        load.wait()

    sub = lax.broadcasted_iota(jnp.int32, (8, 1), 0)
    low = sub < 4
    lane = lax.broadcasted_iota(jnp.int32, (1, 128), 1)

    def start_tile(r, carry):
        at = pl.ds(pl.multiple_of(r * 8, 8), 8)
        m = sea[at, :].astype(F32)
        wet[at, pl.ds(0, COLS)] = m
        for l in range(LEVELS):
            field[l, at, pl.ds(0, COLS)] = mem[l, at, :] * inc[l, at, :] * m
        first = jnp.zeros((8, 128), F32)
        last = jnp.zeros((8, 128), F32)
        left = [field[l, at, pl.ds(0, 128)] for l in range(LEVELS)]
        left += [zon[at, pl.ds(0, 128)], mer[at, pl.ds(0, 128)], m[:, :128]]
        right = [field[l, at, pl.ds(COLS - 128, 128)] for l in range(LEVELS)]
        right += [zon[at, pl.ds(COLS - 128, 128)], mer[at, pl.ds(COLS - 128, 128)], m[:, COLS - 128:]]
        for f in range(7):
            here = (lane >= 4 * f) & (lane < 4 * f + 4)
            a = left[f] if f == 0 else pltpu.roll(left[f], 4 * f, 1)
            b = pltpu.roll(right[f], 4 * f + 4, 1)
            first = jnp.where(here, a, first)
            last = jnp.where(here, b, last)
        cols_out[0, at, :] = first
        cols_out[1, at, :] = last
        return carry

    lax.fori_loop(0, 8, start_tile, 0)

    def tables(at):
        both = [field[l, at, pl.ds(0, COLS)] for l in range(LEVELS)]
        return both + [zon[at, :], mer[at, :], wet[at, pl.ds(0, COLS)]]

    top = tables(pl.ds(0, 8))
    bottom = tables(pl.ds(ROWS - 8, 8))
    for i in range(4):
        if i < 3:
            rows_out[0, i] = jnp.where(low, top[2 * i], pltpu.roll(top[2 * i + 1], 4, 0))
            rows_out[1, i] = jnp.where(low, pltpu.roll(bottom[2 * i + 1], 4, 0), bottom[2 * i])
        else:
            rows_out[0, i] = top[6]
            rows_out[1, i] = bottom[6]

    pl.semaphore_wait(barrier, len(partners))

    def push(src, dst, send, recv, device):
        return pltpu.make_async_remote_copy(
            src_ref=src, dst_ref=dst, send_sem=send, recv_sem=recv,
            device_id=device, device_id_type=MESH,
        )

    halo = [
        push(rows_out.at[0], rows_in.at[0], halo_send.at[0], halo_recv.at[0], beside(-1, 0)),
        push(rows_out.at[1], rows_in.at[1], halo_send.at[1], halo_recv.at[1], beside(1, 0)),
        push(cols_out.at[0], cols_in.at[0], halo_send.at[2], halo_recv.at[2], beside(0, -1)),
        push(cols_out.at[1], cols_in.at[1], halo_send.at[3], halo_recv.at[3], beside(0, 1)),
    ]
    for side in range(2):
        for end in range(2):
            i = side * 2 + end
            halo.append(
                push(
                    cols_out.at[side, pl.ds(end * (ROWS - 8), 8)],
                    corner_in.at[side, end],
                    halo_send.at[4 + i], halo_recv.at[4 + i],
                    beside(-1 if end == 0 else 1, -1 if side == 0 else 1),
                )
            )
    for copy in halo:
        copy.start()
    for copy in halo:
        copy.wait_recv()

    has_after = gy < 3
    has_before = gy > 0
    edge_ok = jnp.where(low, has_after.astype(jnp.int32), has_before.astype(jnp.int32)) > 0

    after_before = []
    for i in range(4):
        n, s = rows_in[0, i], rows_in[1, i]
        after_before.append(jnp.where(edge_ok, jnp.where(low, n, s), 0.0))
        if i < 3:
            swap = pltpu.roll(jnp.where(low, s, n), 4, 0)
            after_before.append(jnp.where(edge_ok, swap, 0.0))
    tail = pl.ds(ROWS, 8)
    for l in range(LEVELS):
        field[l, tail, pl.ds(0, COLS)] = after_before[l]
    wet[tail, pl.ds(0, COLS)] = after_before[6]

    def side_tile(f, right, left):
        a = right if f == 0 else pltpu.roll(right, 128 - 4 * f, 1)
        b = pltpu.roll(left, 124 - 4 * f, 1)
        return jnp.where(lane < 4, a, jnp.where(lane >= 124, b, 0.0))

    def columns(r, carry):
        at = pl.ds(pl.multiple_of(r * 8, 8), 8)
        right, left = cols_in[0, at, :], cols_in[1, at, :]
        for l in range(LEVELS):
            field[l, at, pl.ds(COLS, 128)] = side_tile(l, right, left)
        east[at, pl.ds(COLS, 128)] = side_tile(4, right, left)
        north[at, pl.ds(COLS, 128)] = side_tile(5, right, left)
        wet[at, pl.ds(COLS, 128)] = side_tile(6, right, left)
        east[at, pl.ds(0, COLS)] = zon[at, :]
        north[at, pl.ds(0, COLS)] = mer[at, :]
        return carry

    lax.fori_loop(0, 8, columns, 0)
    right = jnp.where(edge_ok, jnp.where(low, corner_in[0, 0], corner_in[0, 1]), 0.0)
    left = jnp.where(edge_ok, jnp.where(low, corner_in[1, 0], corner_in[1, 1]), 0.0)
    for l in range(LEVELS):
        field[l, tail, pl.ds(COLS, 128)] = side_tile(l, right, left)
    east[tail, pl.ds(COLS, 128)] = side_tile(4, right, left)
    north[tail, pl.ds(COLS, 128)] = side_tile(5, right, left)
    wet[tail, pl.ds(COLS, 128)] = side_tile(6, right, left)
    east[tail, pl.ds(0, COLS)] = after_before[4]
    north[tail, pl.ds(0, COLS)] = after_before[5]

    wide = lax.broadcasted_iota(jnp.int32, (1, XCOLS), 1)
    inside = (wide < COLS + 3) | (wide >= XCOLS - 4)

    def rows_up(ref, r):
        here = pltpu.roll(ref[pl.ds(8 * r, 8), :], 7, 0)
        following = pltpu.roll(ref[pl.ds(8 * ((r + 1) % 9), 8), :], 7, 0)
        return jnp.where(sub == 7, following, here)

    for r in range(9):
        at = pl.ds(8 * r, 8)
        m = wet[at, :]
        east[at, :] = jnp.where(inside, east[at, :] * m * pltpu.roll(m, XCOLS - 1, 1), 0.0)
        weight = north[at, :] * m * rows_up(wet, r)
        if r == 8:
            weight = jnp.where(sub == 3, 0.0, weight)
        north[at, :] = weight

    def level(l, carry):
        for step in range(STEPS):
            src = field.at[l] if step % 2 == 0 else other
            dst = other if step % 2 == 0 else field.at[l]
            last_step = step == STEPS - 1

            def flux(r):
                return north[pl.ds(8 * r, 8), :] * (rows_up(src, r) - src[pl.ds(8 * r, 8), :])

            before = pltpu.roll(flux(8), 1, 0)
            for r in range(8 if last_step else 9):
                at = pl.ds(8 * r, 8)
                u = src[at, :]
                go_east = east[at, :] * (pltpu.roll(u, XCOLS - 1, 1) - u)
                go_west = pltpu.roll(go_east, 1, 1)
                go_north = flux(r)
                down = pltpu.roll(go_north, 1, 0)
                go_south = jnp.where(sub == 0, before, down)
                before = down
                new = u + go_east - go_west + go_north - go_south
                if last_step:
                    term[l, at, :] = mem[l, at, :] * new[:, :COLS]
                else:
                    dst[at, :] = new
        return carry

    my_half = pl.ds(pl.multiple_of(core * HALF, HALF), HALF)
    their_half = pl.ds(pl.multiple_of((1 - core) * HALF, HALF), HALF)
    my_rows = pl.ds(pl.multiple_of(z * 8, 8), 8)

    def core_copy(l):
        return push(term.at[l, :, their_half], peer.at[l], core_send.at[l], core_recv.at[l], core_peer)

    def reduce_copy(l, k):
        to = lax.rem(z + k, 8)
        rows = pl.ds(pl.multiple_of(to * 8, 8), 8)
        return push(part.at[l, rows], gathered.at[k - 1, l], red_send.at[k - 1, l], red_recv.at[k - 1, l], along(k))

    def y_copy(l):
        return push(mine.at[l], across.at[l], y_send.at[l], y_recv.at[l], y_peer)

    def gather_copy(l, k):
        piece = out.at[l, my_rows, my_half]
        return push(piece, piece, ag_send.at[k - 1, l], ag_recv.at[k - 1, l], along(k))

    def forward_copy(l, k):
        source = lax.rem(z + 8 - k, 8)
        piece = out.at[l, pl.ds(pl.multiple_of(source * 8, 8), 8), my_half]
        return push(piece, piece, fwd_send.at[k, l], fwd_recv.at[k, l], core_peer)

    def reduce_level(l):
        core_copy(l).wait_recv()
        part[l] = term[l, :, my_half] + peer[l]
        for k in range(1, 8):
            reduce_copy(l, k).start()

    def compute(l, carry):
        level(l, 0)
        core_copy(l).start()

        @pl.when(l > 0)
        def _():
            reduce_level(l - 1)

        return carry

    lax.fori_loop(0, LEVELS, compute, 0)
    reduce_level(LEVELS - 1)

    def sum_level(l, carry):
        total = part[l, my_rows, :]
        for k in range(1, 8):
            reduce_copy(l, k).wait_recv()
            total = total + gathered[k - 1, l]
        mine[l] = total
        y_copy(l).start()
        return carry

    lax.fori_loop(0, LEVELS, sum_level, 0)

    def share_level(l, carry):
        y_copy(l).wait_recv()
        out[l, my_rows, my_half] = mine[l] + across[l]
        for k in range(1, 8):
            gather_copy(l, k).start()
        forward_copy(l, 0).start()
        return carry

    lax.fori_loop(0, LEVELS, share_level, 0)

    def pass_level(l, carry):
        for k in range(1, 8):
            gather_copy(l, k).wait_recv()
            forward_copy(l, k).start()
        return carry

    lax.fori_loop(0, LEVELS, pass_level, 0)

    def drain(l, carry):
        for k in range(8):
            forward_copy(l, k).wait()
        for k in range(1, 8):
            gather_copy(l, k).wait_send()
            reduce_copy(l, k).wait_send()
        core_copy(l).wait_send()
        y_copy(l).wait_send()
        return carry

    lax.fori_loop(0, LEVELS, drain, 0)
    for copy in halo:
        copy.wait_send()


def shards(increment, members, zonal_diff, merid_diff, sea_mask):
    vmem = pltpu.VMEM
    dma = pltpu.SemaphoreType.DMA
    return pl.pallas_call(
        kernel,
        out_shape=jax.ShapeDtypeStruct((LEVELS, ROWS, COLS), F32),
        in_specs=[pl.BlockSpec(memory_space=pl.ANY)] * 5,
        out_specs=pl.BlockSpec(memory_space=pltpu.VMEM),
        scratch_shapes=[
            vmem((LEVELS, ROWS, COLS), F32),
            vmem((LEVELS, ROWS, COLS), F32),
            vmem((ROWS, COLS), F32),
            vmem((ROWS, COLS), F32),
            vmem((ROWS, COLS), jnp.int32),
            vmem((LEVELS, XROWS, XCOLS), F32),
            vmem((XROWS, XCOLS), F32),
            vmem((XROWS, XCOLS), F32),
            vmem((XROWS, XCOLS), F32),
            vmem((XROWS, XCOLS), F32),
            vmem((2, 4, 8, COLS), F32),
            vmem((2, 4, 8, COLS), F32),
            vmem((2, ROWS, 128), F32),
            vmem((2, ROWS, 128), F32),
            vmem((2, 2, 8, 128), F32),
            vmem((LEVELS, ROWS, COLS), F32),
            vmem((LEVELS, ROWS, HALF), F32),
            vmem((LEVELS, ROWS, HALF), F32),
            vmem((7, LEVELS, 8, HALF), F32),
            vmem((LEVELS, 8, HALF), F32),
            vmem((LEVELS, 8, HALF), F32),
            dma((5,)),
            dma((8,)), dma((8,)),
            dma((LEVELS,)), dma((LEVELS,)),
            dma((7, LEVELS)), dma((7, LEVELS)),
            dma((LEVELS,)), dma((LEVELS,)),
            dma((7, LEVELS)), dma((7, LEVELS)),
            dma((8, LEVELS)), dma((8, LEVELS)),
        ],
        compiler_params=pltpu.CompilerParams(collective_id=0, has_side_effects=True),
    )(increment, members, zonal_diff, merid_diff, sea_mask)


def solution(mesh):
    return jax.shard_map(
        shards,
        mesh=mesh,
        in_specs=(
            P(None, "gy", "gx"),
            P("mem", None, "gy", "gx"),
            P("gy", "gx"),
            P("gy", "gx"),
            P("gy", "gx"),
        ),
        out_specs=P(None, "gy", "gx"),
        check_vma=False,
    )
```

```python
import jax
import jax.numpy as jnp
from jax import lax
from jax.experimental import pallas as pl
from jax.experimental.pallas import tpu as pltpu
from jax.sharding import PartitionSpec as P

STEPS = 4
LEVELS = 4
ROWS = 64
COLS = 1024
XROWS = ROWS + 8
XCOLS = COLS + 128
HALF = COLS // 2
MESH = pl.DeviceIdType.MESH
F32 = jnp.float32


def kernel(
    inc_hbm, mem_hbm, zon_hbm, mer_hbm, sea_hbm, out,
    inc, mem, zon, mer, sea,
    field, other, wet, east, west, north, south,
    rows_out, rows_in, cols_out, cols_in, corner_in,
    term, peer, part, near, far, split, joint, joined, mine, across,
    load_sem, halo_send, halo_recv, core_send, core_recv,
    red_send, red_recv, join_send, join_recv, y_send, y_recv, ag_send, ag_recv, fwd_send, fwd_recv,
):
    me = lax.axis_index("mem")
    gy = lax.axis_index("gy")
    gx = lax.axis_index("gx")
    z = me // 4
    hi = lax.rem(me // 2, 2)
    core = lax.rem(me, 2)

    def member_at(z_, hi_, core_):
        return z_ * 4 + hi_ * 2 + core_

    def beside(dy, dx):
        y = lax.rem(hi * 4 + gy + dy + 8, 8)
        return (member_at(z, y // 4, core), lax.rem(y, 4), lax.rem(gx + dx + 4, 4))

    def along(k):
        return (member_at(lax.rem(z + k + 8, 8), hi, core), gy, gx)

    core_peer = (member_at(z, hi, 1 - core), gy, gx)
    y_peer = (member_at(z, 1 - hi, core), gy, gx)

    barrier = pltpu.get_barrier_semaphore()
    around = [(-1, 0), (1, 0), (0, -1), (0, 1), (-1, -1), (1, -1), (-1, 1), (1, 1)]
    partners = [beside(dy, dx) for dy, dx in around]
    partners += [core_peer, y_peer] + [along(k) for k in range(1, 8)]
    for device in partners:
        pl.semaphore_signal(barrier, inc=1, device_id=device, device_id_type=MESH)

    loads = [
        pltpu.make_async_copy(sea_hbm, sea, load_sem.at[0]),
        pltpu.make_async_copy(zon_hbm, zon, load_sem.at[1]),
        pltpu.make_async_copy(mer_hbm, mer, load_sem.at[2]),
        pltpu.make_async_copy(inc_hbm, inc, load_sem.at[3]),
        pltpu.make_async_copy(mem_hbm.at[0], mem, load_sem.at[4]),
    ]
    for load in loads:
        load.start()
    for load in loads:
        load.wait()

    sub = lax.broadcasted_iota(jnp.int32, (8, 1), 0)
    low = sub < 4
    lane = lax.broadcasted_iota(jnp.int32, (1, 128), 1)

    def start_tile(r, carry):
        at = pl.ds(pl.multiple_of(r * 8, 8), 8)
        m = sea[at, :].astype(F32)
        wet[at, pl.ds(0, COLS)] = m
        for l in range(LEVELS):
            field[l, at, pl.ds(0, COLS)] = mem[l, at, :] * inc[l, at, :] * m
        first = jnp.zeros((8, 128), F32)
        last = jnp.zeros((8, 128), F32)
        left = [field[l, at, pl.ds(0, 128)] for l in range(LEVELS)]
        left += [zon[at, pl.ds(0, 128)], mer[at, pl.ds(0, 128)], m[:, :128]]
        right = [field[l, at, pl.ds(COLS - 128, 128)] for l in range(LEVELS)]
        right += [zon[at, pl.ds(COLS - 128, 128)], mer[at, pl.ds(COLS - 128, 128)], m[:, COLS - 128:]]
        for f in range(7):
            here = (lane >= 4 * f) & (lane < 4 * f + 4)
            a = left[f] if f == 0 else pltpu.roll(left[f], 4 * f, 1)
            b = pltpu.roll(right[f], 4 * f + 4, 1)
            first = jnp.where(here, a, first)
            last = jnp.where(here, b, last)
        cols_out[0, at, :] = first
        cols_out[1, at, :] = last
        return carry

    lax.fori_loop(0, 8, start_tile, 0)

    def tables(at):
        both = [field[l, at, pl.ds(0, COLS)] for l in range(LEVELS)]
        return both + [zon[at, :], mer[at, :], wet[at, pl.ds(0, COLS)]]

    top = tables(pl.ds(0, 8))
    bottom = tables(pl.ds(ROWS - 8, 8))
    for i in range(4):
        if i < 3:
            rows_out[0, i] = jnp.where(low, top[2 * i], pltpu.roll(top[2 * i + 1], 4, 0))
            rows_out[1, i] = jnp.where(low, pltpu.roll(bottom[2 * i + 1], 4, 0), bottom[2 * i])
        else:
            rows_out[0, i] = top[6]
            rows_out[1, i] = bottom[6]

    pl.semaphore_wait(barrier, len(partners))

    def push(src, dst, send, recv, device):
        return pltpu.make_async_remote_copy(
            src_ref=src, dst_ref=dst, send_sem=send, recv_sem=recv,
            device_id=device, device_id_type=MESH,
        )

    halo = [
        push(rows_out.at[0], rows_in.at[0], halo_send.at[0], halo_recv.at[0], beside(-1, 0)),
        push(rows_out.at[1], rows_in.at[1], halo_send.at[1], halo_recv.at[1], beside(1, 0)),
        push(cols_out.at[0], cols_in.at[0], halo_send.at[2], halo_recv.at[2], beside(0, -1)),
        push(cols_out.at[1], cols_in.at[1], halo_send.at[3], halo_recv.at[3], beside(0, 1)),
    ]
    for side in range(2):
        for end in range(2):
            i = side * 2 + end
            halo.append(
                push(
                    cols_out.at[side, pl.ds(end * (ROWS - 8), 8)],
                    corner_in.at[side, end],
                    halo_send.at[4 + i], halo_recv.at[4 + i],
                    beside(-1 if end == 0 else 1, -1 if side == 0 else 1),
                )
            )
    for copy in halo:
        copy.start()
    for copy in halo:
        copy.wait_recv()

    has_after = gy < 3
    has_before = gy > 0
    edge_ok = jnp.where(low, has_after.astype(jnp.int32), has_before.astype(jnp.int32)) > 0

    after_before = []
    for i in range(4):
        n, s = rows_in[0, i], rows_in[1, i]
        after_before.append(jnp.where(edge_ok, jnp.where(low, n, s), 0.0))
        if i < 3:
            swap = pltpu.roll(jnp.where(low, s, n), 4, 0)
            after_before.append(jnp.where(edge_ok, swap, 0.0))
    tail = pl.ds(ROWS, 8)
    for l in range(LEVELS):
        field[l, tail, pl.ds(0, COLS)] = after_before[l]
    wet[tail, pl.ds(0, COLS)] = after_before[6]

    def side_tile(f, right, left):
        a = right if f == 0 else pltpu.roll(right, 128 - 4 * f, 1)
        b = pltpu.roll(left, 124 - 4 * f, 1)
        return jnp.where(lane < 4, a, jnp.where(lane >= 124, b, 0.0))

    def columns(r, carry):
        at = pl.ds(pl.multiple_of(r * 8, 8), 8)
        right, left = cols_in[0, at, :], cols_in[1, at, :]
        for l in range(LEVELS):
            field[l, at, pl.ds(COLS, 128)] = side_tile(l, right, left)
        east[at, pl.ds(COLS, 128)] = side_tile(4, right, left)
        north[at, pl.ds(COLS, 128)] = side_tile(5, right, left)
        wet[at, pl.ds(COLS, 128)] = side_tile(6, right, left)
        east[at, pl.ds(0, COLS)] = zon[at, :]
        north[at, pl.ds(0, COLS)] = mer[at, :]
        return carry

    lax.fori_loop(0, 8, columns, 0)
    right = jnp.where(edge_ok, jnp.where(low, corner_in[0, 0], corner_in[0, 1]), 0.0)
    left = jnp.where(edge_ok, jnp.where(low, corner_in[1, 0], corner_in[1, 1]), 0.0)
    for l in range(LEVELS):
        field[l, tail, pl.ds(COLS, 128)] = side_tile(l, right, left)
    east[tail, pl.ds(COLS, 128)] = side_tile(4, right, left)
    north[tail, pl.ds(COLS, 128)] = side_tile(5, right, left)
    wet[tail, pl.ds(COLS, 128)] = side_tile(6, right, left)
    east[tail, pl.ds(0, COLS)] = after_before[4]
    north[tail, pl.ds(0, COLS)] = after_before[5]

    wide = lax.broadcasted_iota(jnp.int32, (1, XCOLS), 1)
    inside = (wide < COLS + 3) | (wide >= XCOLS - 4)

    def rows_up(ref, r):
        here = pltpu.roll(ref[pl.ds(8 * r, 8), :], 7, 0)
        following = pltpu.roll(ref[pl.ds(8 * ((r + 1) % 9), 8), :], 7, 0)
        return jnp.where(sub == 7, following, here)

    def rows_down(ref, r):
        here = pltpu.roll(ref[pl.ds(8 * r, 8), :], 1, 0)
        preceding = pltpu.roll(ref[pl.ds(8 * ((r + 8) % 9), 8), :], 1, 0)
        return jnp.where(sub == 0, preceding, here)

    for r in range(9):
        at = pl.ds(8 * r, 8)
        m = wet[at, :]
        weight = jnp.where(inside, east[at, :] * m * pltpu.roll(m, XCOLS - 1, 1), 0.0)
        east[at, :] = weight
        west[at, :] = pltpu.roll(weight, 1, 1)
        weight = north[at, :] * m * rows_up(wet, r)
        if r == 8:
            weight = jnp.where(sub == 3, 0.0, weight)
        north[at, :] = weight
    for r in range(9):
        south[pl.ds(8 * r, 8), :] = rows_down(north, r)

    def level(l, carry):
        for step in range(STEPS):
            src = field.at[l] if step % 2 == 0 else other
            dst = other if step % 2 == 0 else field.at[l]
            last_step = step == STEPS - 1

            for r in range(8 if last_step else 9):
                at = pl.ds(8 * r, 8)
                u = src[at, :]
                go_east = east[at, :] * (pltpu.roll(u, XCOLS - 1, 1) - u)
                go_west = west[at, :] * (u - pltpu.roll(u, 1, 1))
                go_north = north[at, :] * (rows_up(src, r) - u)
                go_south = south[at, :] * (u - rows_down(src, r))
                new = u + go_east - go_west + go_north - go_south
                if last_step:
                    term[l, at, :] = mem[l, at, :] * new[:, :COLS]
                else:
                    dst[at, :] = new
        return carry

    my_half = pl.ds(pl.multiple_of(core * HALF, HALF), HALF)
    their_half = pl.ds(pl.multiple_of((1 - core) * HALF, HALF), HALF)
    my_rows = pl.ds(pl.multiple_of(z * 8, 8), 8)

    def core_copy(l):
        return push(term.at[l, :, their_half], peer.at[l], core_send.at[l], core_recv.at[l], core_peer)

    def rows_of(k):
        return pl.ds(pl.multiple_of(lax.rem(z + k + 8, 8) * 8, 8), 8)

    def first_copies(l):
        copies = []
        for side, sign in enumerate((1, -1)):
            cut = pl.ds(side * (HALF // 2), HALF // 2)
            for i, (src, dst, to) in enumerate((
                (part.at[l, rows_of(3 * sign)], far.at[side, l], sign),
                (part.at[l, rows_of(4), cut], split.at[side, l], 2 * sign),
                (part.at[l, rows_of(sign)], near.at[side, l], sign),
            )):
                at = side * 3 + i
                copies.append(push(src, dst, red_send.at[at, l], red_recv.at[at, l], along(to)))
        return copies

    def second_copies(l):
        return [
            push(joint.at[side, l], joined.at[side, l], join_send.at[side, l], join_recv.at[side, l], along(2 * sign))
            for side, sign in enumerate((1, -1))
        ]

    def y_copy(l):
        return push(mine.at[l], across.at[l], y_send.at[l], y_recv.at[l], y_peer)

    def gather_copy(l, k):
        piece = out.at[l, my_rows, my_half]
        return push(piece, piece, ag_send.at[k - 1, l], ag_recv.at[k - 1, l], along(k))

    def forward_copy(l, k):
        source = lax.rem(z + 8 - k, 8)
        piece = out.at[l, pl.ds(pl.multiple_of(source * 8, 8), 8), my_half]
        return push(piece, piece, fwd_send.at[k, l], fwd_recv.at[k, l], core_peer)

    def reduce_level(l):
        core_copy(l).wait_recv()
        part[l] = term[l, :, my_half] + peer[l]
        for copy in first_copies(l):
            copy.start()

    def compute(l, carry):
        level(l, 0)
        core_copy(l).start()

        @pl.when(l > 0)
        def _():
            reduce_level(l - 1)

        return carry

    lax.fori_loop(0, LEVELS, compute, 0)
    reduce_level(LEVELS - 1)

    def join_level(l, carry):
        first = first_copies(l)
        second = second_copies(l)
        for side, sign in enumerate((1, -1)):
            first[side * 3].wait_recv()
            first[side * 3 + 1].wait_recv()
            joint[side, l] = part[l, rows_of(2 * sign), :] + far[side, l]
            cut = pl.ds(side * (HALF // 2), HALF // 2)
            joint[side, l, :, cut] = joint[side, l, :, cut] + split[side, l]
            second[side].start()
        return carry

    lax.fori_loop(0, LEVELS, join_level, 0)

    def sum_level(l, carry):
        first = first_copies(l)
        second = second_copies(l)
        for side in range(2):
            first[side * 3 + 2].wait_recv()
            second[side].wait_recv()
        total = part[l, my_rows, :] + near[0, l] + near[1, l]
        mine[l] = total + joined[0, l] + joined[1, l]
        y_copy(l).start()
        return carry

    lax.fori_loop(0, LEVELS, sum_level, 0)

    def share_level(l, carry):
        y_copy(l).wait_recv()
        out[l, my_rows, my_half] = mine[l] + across[l]
        forward_copy(l, 0).start()

        def send(to, c):
            @pl.when(to != z)
            def _():
                gather_copy(l, lax.rem(to - z + 8, 8)).start()
            return c

        lax.fori_loop(0, 8, send, 0)
        return carry

    lax.fori_loop(0, LEVELS, share_level, 0)

    def pass_level(l, carry):
        for k in range(1, 8):
            gather_copy(l, k).wait_recv()
            forward_copy(l, k).start()
        return carry

    lax.fori_loop(0, LEVELS, pass_level, 0)

    def drain(l, carry):
        for k in range(8):
            forward_copy(l, k).wait()
        for k in range(1, 8):
            gather_copy(l, k).wait_send()
        for copy in first_copies(l) + second_copies(l):
            copy.wait_send()
        core_copy(l).wait_send()
        y_copy(l).wait_send()
        return carry

    lax.fori_loop(0, LEVELS, drain, 0)
    for copy in halo:
        copy.wait_send()


def shards(increment, members, zonal_diff, merid_diff, sea_mask):
    vmem = pltpu.VMEM
    dma = pltpu.SemaphoreType.DMA
    return pl.pallas_call(
        kernel,
        out_shape=pltpu.VMEM((LEVELS, ROWS, COLS), F32),
        in_specs=[pl.BlockSpec(memory_space=pl.ANY)] * 5,
        out_specs=pl.BlockSpec(memory_space=pltpu.VMEM),
        scratch_shapes=[
            vmem((LEVELS, ROWS, COLS), F32),
            vmem((LEVELS, ROWS, COLS), F32),
            vmem((ROWS, COLS), F32),
            vmem((ROWS, COLS), F32),
            vmem((ROWS, COLS), jnp.int32),
            vmem((LEVELS, XROWS, XCOLS), F32),
            vmem((XROWS, XCOLS), F32),
            vmem((XROWS, XCOLS), F32),
            vmem((XROWS, XCOLS), F32),
            vmem((XROWS, XCOLS), F32),
            vmem((XROWS, XCOLS), F32),
            vmem((XROWS, XCOLS), F32),
            vmem((2, 4, 8, COLS), F32),
            vmem((2, 4, 8, COLS), F32),
            vmem((2, ROWS, 128), F32),
            vmem((2, ROWS, 128), F32),
            vmem((2, 2, 8, 128), F32),
            vmem((LEVELS, ROWS, COLS), F32),
            vmem((LEVELS, ROWS, HALF), F32),
            vmem((LEVELS, ROWS, HALF), F32),
            vmem((2, LEVELS, 8, HALF), F32),
            vmem((2, LEVELS, 8, HALF), F32),
            vmem((2, LEVELS, 8, HALF // 2), F32),
            vmem((2, LEVELS, 8, HALF), F32),
            vmem((2, LEVELS, 8, HALF), F32),
            vmem((LEVELS, 8, HALF), F32),
            vmem((LEVELS, 8, HALF), F32),
            dma((5,)),
            dma((8,)), dma((8,)),
            dma((LEVELS,)), dma((LEVELS,)),
            dma((6, LEVELS)), dma((6, LEVELS)),
            dma((2, LEVELS)), dma((2, LEVELS)),
            dma((LEVELS,)), dma((LEVELS,)),
            dma((7, LEVELS)), dma((7, LEVELS)),
            dma((8, LEVELS)), dma((8, LEVELS)),
        ],
        compiler_params=pltpu.CompilerParams(collective_id=0, has_side_effects=True),
    )(increment, members, zonal_diff, merid_diff, sea_mask)


def solution(mesh):
    return jax.shard_map(
        shards,
        mesh=mesh,
        in_specs=(
            P(None, "gy", "gx"),
            P("mem", None, "gy", "gx"),
            P("gy", "gx"),
            P("gy", "gx"),
            P("gy", "gx"),
        ),
        out_specs=P(None, "gy", "gx"),
        check_vma=False,
    )
```

```python
import jax
import jax.numpy as jnp
from jax import lax
from jax.experimental import pallas as pl
from jax.experimental.pallas import tpu as pltpu
from jax.sharding import PartitionSpec as P

STEPS = 4
LEVELS = 4
ROWS = 64
COLS = 1024
XROWS = ROWS + 8
XCOLS = COLS + 128
HALF = COLS // 2
EAGER = 0
SOON = 2
MESH = pl.DeviceIdType.MESH
F32 = jnp.float32


def kernel(
    inc_hbm, mem_hbm, zon_hbm, mer_hbm, sea_hbm, out,
    inc, mem, zon, mer, sea,
    field, other, wet, east, west, north, south,
    rows_out, rows_in, cols_out, cols_in, corner_in,
    term, peer, part, near, far, split, joint, joined, mine, across,
    load_sem, halo_send, halo_recv, core_send, core_recv,
    red_send, red_recv, join_send, join_recv, y_send, y_recv, ag_send, ag_recv, relay_send, fwd_send, fwd_recv,
):
    me = lax.axis_index("mem")
    gy = lax.axis_index("gy")
    gx = lax.axis_index("gx")
    z = me // 4
    hi = lax.rem(me // 2, 2)
    core = lax.rem(me, 2)

    def member_at(z_, hi_, core_):
        return z_ * 4 + hi_ * 2 + core_

    def beside(dy, dx):
        y = lax.rem(hi * 4 + gy + dy + 8, 8)
        return (member_at(z, y // 4, core), lax.rem(y, 4), lax.rem(gx + dx + 4, 4))

    def along(k):
        return (member_at(lax.rem(z + k + 8, 8), hi, core), gy, gx)

    core_peer = (member_at(z, hi, 1 - core), gy, gx)
    y_peer = (member_at(z, 1 - hi, core), gy, gx)

    barrier = pltpu.get_barrier_semaphore()
    around = [(-1, 0), (1, 0), (0, -1), (0, 1), (-1, -1), (1, -1), (-1, 1), (1, 1)]
    partners = [beside(dy, dx) for dy, dx in around]
    partners += [core_peer, y_peer] + [along(k) for k in range(1, 8)]
    for device in partners:
        pl.semaphore_signal(barrier, inc=1, device_id=device, device_id_type=MESH)

    loads = [
        pltpu.make_async_copy(sea_hbm, sea, load_sem.at[0]),
        pltpu.make_async_copy(zon_hbm, zon, load_sem.at[1]),
        pltpu.make_async_copy(mer_hbm, mer, load_sem.at[2]),
        pltpu.make_async_copy(inc_hbm, inc, load_sem.at[3]),
        pltpu.make_async_copy(mem_hbm.at[0], mem, load_sem.at[4]),
    ]
    for load in loads:
        load.start()
    for load in loads:
        load.wait()

    sub = lax.broadcasted_iota(jnp.int32, (8, 1), 0)
    low = sub < 4
    lane = lax.broadcasted_iota(jnp.int32, (1, 128), 1)

    def start_tile(r, carry):
        at = pl.ds(pl.multiple_of(r * 8, 8), 8)
        m = sea[at, :].astype(F32)
        wet[at, pl.ds(0, COLS)] = m
        for l in range(LEVELS):
            field[l, at, pl.ds(0, COLS)] = mem[l, at, :] * inc[l, at, :] * m
        first = jnp.zeros((8, 128), F32)
        last = jnp.zeros((8, 128), F32)
        left = [field[l, at, pl.ds(0, 128)] for l in range(LEVELS)]
        left += [zon[at, pl.ds(0, 128)], mer[at, pl.ds(0, 128)], m[:, :128]]
        right = [field[l, at, pl.ds(COLS - 128, 128)] for l in range(LEVELS)]
        right += [zon[at, pl.ds(COLS - 128, 128)], mer[at, pl.ds(COLS - 128, 128)], m[:, COLS - 128:]]
        for f in range(7):
            here = (lane >= 4 * f) & (lane < 4 * f + 4)
            a = left[f] if f == 0 else pltpu.roll(left[f], 4 * f, 1)
            b = pltpu.roll(right[f], 4 * f + 4, 1)
            first = jnp.where(here, a, first)
            last = jnp.where(here, b, last)
        cols_out[0, at, :] = first
        cols_out[1, at, :] = last
        return carry

    lax.fori_loop(0, 8, start_tile, 0)

    def tables(at):
        both = [field[l, at, pl.ds(0, COLS)] for l in range(LEVELS)]
        return both + [zon[at, :], mer[at, :], wet[at, pl.ds(0, COLS)]]

    top = tables(pl.ds(0, 8))
    bottom = tables(pl.ds(ROWS - 8, 8))
    for i in range(4):
        if i < 3:
            rows_out[0, i] = jnp.where(low, top[2 * i], pltpu.roll(top[2 * i + 1], 4, 0))
            rows_out[1, i] = jnp.where(low, pltpu.roll(bottom[2 * i + 1], 4, 0), bottom[2 * i])
        else:
            rows_out[0, i] = top[6]
            rows_out[1, i] = bottom[6]

    pl.semaphore_wait(barrier, len(partners))

    def push(src, dst, send, recv, device):
        return pltpu.make_async_remote_copy(
            src_ref=src, dst_ref=dst, send_sem=send, recv_sem=recv,
            device_id=device, device_id_type=MESH,
        )

    halo = [
        push(rows_out.at[0], rows_in.at[0], halo_send.at[0], halo_recv.at[0], beside(-1, 0)),
        push(rows_out.at[1], rows_in.at[1], halo_send.at[1], halo_recv.at[1], beside(1, 0)),
        push(cols_out.at[0], cols_in.at[0], halo_send.at[2], halo_recv.at[2], beside(0, -1)),
        push(cols_out.at[1], cols_in.at[1], halo_send.at[3], halo_recv.at[3], beside(0, 1)),
    ]
    for side in range(2):
        for end in range(2):
            i = side * 2 + end
            halo.append(
                push(
                    cols_out.at[side, pl.ds(end * (ROWS - 8), 8)],
                    corner_in.at[side, end],
                    halo_send.at[4 + i], halo_recv.at[4 + i],
                    beside(-1 if end == 0 else 1, -1 if side == 0 else 1),
                )
            )
    for copy in halo[::-1]:
        copy.start()
    for copy in halo:
        copy.wait_recv()

    has_after = gy < 3
    has_before = gy > 0
    edge_ok = jnp.where(low, has_after.astype(jnp.int32), has_before.astype(jnp.int32)) > 0

    after_before = []
    for i in range(4):
        n, s = rows_in[0, i], rows_in[1, i]
        after_before.append(jnp.where(edge_ok, jnp.where(low, n, s), 0.0))
        if i < 3:
            swap = pltpu.roll(jnp.where(low, s, n), 4, 0)
            after_before.append(jnp.where(edge_ok, swap, 0.0))
    tail = pl.ds(ROWS, 8)
    for l in range(LEVELS):
        field[l, tail, pl.ds(0, COLS)] = after_before[l]
    wet[tail, pl.ds(0, COLS)] = after_before[6]

    def side_tile(f, right, left):
        a = right if f == 0 else pltpu.roll(right, 128 - 4 * f, 1)
        b = pltpu.roll(left, 124 - 4 * f, 1)
        return jnp.where(lane < 4, a, jnp.where(lane >= 124, b, 0.0))

    def columns(r, carry):
        at = pl.ds(pl.multiple_of(r * 8, 8), 8)
        right, left = cols_in[0, at, :], cols_in[1, at, :]
        for l in range(LEVELS):
            field[l, at, pl.ds(COLS, 128)] = side_tile(l, right, left)
        east[at, pl.ds(COLS, 128)] = side_tile(4, right, left)
        north[at, pl.ds(COLS, 128)] = side_tile(5, right, left)
        wet[at, pl.ds(COLS, 128)] = side_tile(6, right, left)
        east[at, pl.ds(0, COLS)] = zon[at, :]
        north[at, pl.ds(0, COLS)] = mer[at, :]
        return carry

    lax.fori_loop(0, 8, columns, 0)
    right = jnp.where(edge_ok, jnp.where(low, corner_in[0, 0], corner_in[0, 1]), 0.0)
    left = jnp.where(edge_ok, jnp.where(low, corner_in[1, 0], corner_in[1, 1]), 0.0)
    for l in range(LEVELS):
        field[l, tail, pl.ds(COLS, 128)] = side_tile(l, right, left)
    east[tail, pl.ds(COLS, 128)] = side_tile(4, right, left)
    north[tail, pl.ds(COLS, 128)] = side_tile(5, right, left)
    wet[tail, pl.ds(COLS, 128)] = side_tile(6, right, left)
    east[tail, pl.ds(0, COLS)] = after_before[4]
    north[tail, pl.ds(0, COLS)] = after_before[5]

    wide = lax.broadcasted_iota(jnp.int32, (1, XCOLS), 1)
    inside = (wide < COLS + 3) | (wide >= XCOLS - 4)

    def rows_up(ref, r):
        here = pltpu.roll(ref[pl.ds(8 * r, 8), :], 7, 0)
        following = pltpu.roll(ref[pl.ds(8 * ((r + 1) % 9), 8), :], 7, 0)
        return jnp.where(sub == 7, following, here)

    def rows_down(ref, r):
        here = pltpu.roll(ref[pl.ds(8 * r, 8), :], 1, 0)
        preceding = pltpu.roll(ref[pl.ds(8 * ((r + 8) % 9), 8), :], 1, 0)
        return jnp.where(sub == 0, preceding, here)

    for r in range(9):
        at = pl.ds(8 * r, 8)
        m = wet[at, :]
        weight = jnp.where(inside, east[at, :] * m * pltpu.roll(m, XCOLS - 1, 1), 0.0)
        east[at, :] = weight
        west[at, :] = pltpu.roll(weight, 1, 1)
        weight = north[at, :] * m * rows_up(wet, r)
        if r == 8:
            weight = jnp.where(sub == 3, 0.0, weight)
        north[at, :] = weight
    for r in range(9):
        south[pl.ds(8 * r, 8), :] = rows_down(north, r)

    def level(l, carry):
        for step in range(STEPS):
            src = field.at[l] if step % 2 == 0 else other
            dst = other if step % 2 == 0 else field.at[l]
            last_step = step == STEPS - 1

            for r in range(8 if last_step else 9):
                at = pl.ds(8 * r, 8)
                u = src[at, :]
                go_east = east[at, :] * (pltpu.roll(u, XCOLS - 1, 1) - u)
                go_west = west[at, :] * (u - pltpu.roll(u, 1, 1))
                go_north = north[at, :] * (rows_up(src, r) - u)
                go_south = south[at, :] * (u - rows_down(src, r))
                new = u + go_east - go_west + go_north - go_south
                if last_step:
                    term[l, at, :] = mem[l, at, :] * new[:, :COLS]
                else:
                    dst[at, :] = new
        return carry

    my_half = pl.ds(pl.multiple_of(core * HALF, HALF), HALF)
    their_half = pl.ds(pl.multiple_of((1 - core) * HALF, HALF), HALF)
    my_rows = pl.ds(pl.multiple_of(z * 8, 8), 8)

    def core_copy(l):
        return push(term.at[l, :, their_half], peer.at[l], core_send.at[l], core_recv.at[l], core_peer)

    def rows_of(k):
        return pl.ds(pl.multiple_of(lax.rem(z + k + 8, 8) * 8, 8), 8)

    def first_copies(l):
        copies = []
        for side, sign in enumerate((1, -1)):
            cut = pl.ds(side * (HALF // 2), HALF // 2)
            for i, (src, dst, to) in enumerate((
                (part.at[l, rows_of(3 * sign)], far.at[side, l], sign),
                (part.at[l, rows_of(4), cut], split.at[side, l], 2 * sign),
                (part.at[l, rows_of(sign)], near.at[side, l], sign),
            )):
                at = side * 3 + i
                copies.append(push(src, dst, red_send.at[at, l], red_recv.at[at, l], along(to)))
        return copies

    def second_copies(l):
        return [
            push(joint.at[side, l], joined.at[side, l], join_send.at[side, l], join_recv.at[side, l], along(2 * sign))
            for side, sign in enumerate((1, -1))
        ]

    def y_copy(l):
        return push(mine.at[l], across.at[l], y_send.at[l], y_recv.at[l], y_peer)

    QUARTER = HALF // 2

    def piece_of(l, source, part_):
        start = core * HALF
        if part_ is None:
            where = pl.ds(pl.multiple_of(start, HALF), HALF)
        else:
            where = pl.ds(pl.multiple_of(start + part_ * QUARTER, QUARTER), QUARTER)
        rows = pl.ds(pl.multiple_of(source * 8, 8), 8)
        return out.at[l, rows, where]

    def gather_copies(l, k):
        if k == 4:
            slots = [(3, 0), (7, 1)]
        else:
            slots = [(k - 1, None)]
        copies = []
        for slot, part_ in slots:
            piece = piece_of(l, z, part_)
            copies.append(push(piece, piece, ag_send.at[slot, l], ag_recv.at[slot, l], along(k)))
        return copies

    def soon(k):
        return lax.rem(z + k + 8, 8) < SOON

    def each_owned(l, act, early, late):
        for k in range(1, 8):
            def run(k=k):
                for copy in gather_copies(l, k):
                    act(copy)

            if early:
                pl.when(soon(k))(run)
            if late and k in (1, 2, 6, 7):
                pl.when(jnp.logical_not(soon(k)))(run)

    def relay_copies(l, side):
        sign = 1 - 2 * side
        source = lax.rem(z - 2 * sign + 8, 8)
        whole = piece_of(l, source, None)
        half = piece_of(l, source, side)
        slot = 2 if side == 0 else 4
        half_slot = 3 if side == 0 else 7
        return [
            (sign, push(whole, whole, relay_send.at[2 * side, l], ag_recv.at[slot, l], along(sign))),
            (2 * sign, push(half, half, relay_send.at[2 * side + 1, l], ag_recv.at[half_slot, l], along(2 * sign))),
        ]

    def each_relay(l, side, act):
        for to, copy in relay_copies(l, side):
            @pl.when(jnp.logical_not(soon(to)))
            def _(copy=copy):
                act(copy)

    def arrived(l, k):
        for copy in gather_copies(l, k):
            copy.wait_recv()

    def forward_copy(l, k):
        source = lax.rem(z + 8 - k, 8)
        piece = out.at[l, pl.ds(pl.multiple_of(source * 8, 8), 8), my_half]
        return push(piece, piece, fwd_send.at[k, l], fwd_recv.at[k, l], core_peer)

    def reduce_level(l):
        core_copy(l).wait_recv()
        part[l] = term[l, :, my_half] + peer[l]
        for copy in first_copies(l):
            copy.start()

    def compute(l, carry):
        level(l, 0)
        core_copy(l).start()

        @pl.when(l > 0)
        def _():
            reduce_level(l - 1)

        return carry

    lax.fori_loop(0, LEVELS, compute, 0)
    reduce_level(LEVELS - 1)

    def join_level(l, carry):
        first = first_copies(l)
        second = second_copies(l)
        for side, sign in enumerate((1, -1)):
            first[side * 3].wait_recv()
            first[side * 3 + 1].wait_recv()
            joint[side, l] = part[l, rows_of(2 * sign), :] + far[side, l]
            cut = pl.ds(side * (HALF // 2), HALF // 2)
            joint[side, l, :, cut] = joint[side, l, :, cut] + split[side, l]
            second[side].start()
        return carry

    lax.fori_loop(0, LEVELS, join_level, 0)

    def sum_level(l, carry):
        first = first_copies(l)
        second = second_copies(l)
        for side in range(2):
            first[side * 3 + 2].wait_recv()
            second[side].wait_recv()
        total = part[l, my_rows, :] + near[0, l] + near[1, l]
        mine[l] = total + joined[0, l] + joined[1, l]
        y_copy(l).start()
        return carry

    lax.fori_loop(0, LEVELS, sum_level, 0)

    def share_level(l, carry):
        y_copy(l).wait_recv()
        out[l, my_rows, my_half] = mine[l] + across[l]
        each_owned(l, lambda copy: copy.start(), True, False)
        forward_copy(l, 0).start()

        @pl.when(l < EAGER)
        def _():
            each_owned(l, lambda copy: copy.start(), False, True)

        return carry

    def later_level(l, carry):
        each_owned(l, lambda copy: copy.start(), False, True)
        return carry

    lax.fori_loop(0, LEVELS, share_level, 0)
    lax.fori_loop(EAGER, LEVELS, later_level, 0)

    def pass_level(l, carry):
        for side, k in enumerate((2, 6)):
            arrived(l, k)
            each_relay(l, side, lambda copy: copy.start())
            forward_copy(l, k).start()
        for k in (1, 7):
            arrived(l, k)
            forward_copy(l, k).start()
        return carry

    def far_level(l, carry):
        for k in (3, 5, 4):
            arrived(l, k)
            forward_copy(l, k).start()
        return carry

    lax.fori_loop(0, LEVELS, pass_level, 0)
    lax.fori_loop(0, LEVELS, far_level, 0)

    def drain(l, carry):
        for k in range(8):
            forward_copy(l, k).wait()
        each_owned(l, lambda copy: copy.wait_send(), True, True)
        for side in range(2):
            each_relay(l, side, lambda copy: copy.wait_send())
        for copy in first_copies(l) + second_copies(l):
            copy.wait_send()
        core_copy(l).wait_send()
        y_copy(l).wait_send()
        return carry

    lax.fori_loop(0, LEVELS, drain, 0)
    for copy in halo:
        copy.wait_send()


def shards(increment, members, zonal_diff, merid_diff, sea_mask):
    vmem = pltpu.VMEM
    dma = pltpu.SemaphoreType.DMA
    return pl.pallas_call(
        kernel,
        out_shape=pltpu.VMEM((LEVELS, ROWS, COLS), F32),
        in_specs=[pl.BlockSpec(memory_space=pl.ANY)] * 5,
        out_specs=pl.BlockSpec(memory_space=pltpu.VMEM),
        scratch_shapes=[
            vmem((LEVELS, ROWS, COLS), F32),
            vmem((LEVELS, ROWS, COLS), F32),
            vmem((ROWS, COLS), F32),
            vmem((ROWS, COLS), F32),
            vmem((ROWS, COLS), jnp.int32),
            vmem((LEVELS, XROWS, XCOLS), F32),
            vmem((XROWS, XCOLS), F32),
            vmem((XROWS, XCOLS), F32),
            vmem((XROWS, XCOLS), F32),
            vmem((XROWS, XCOLS), F32),
            vmem((XROWS, XCOLS), F32),
            vmem((XROWS, XCOLS), F32),
            vmem((2, 4, 8, COLS), F32),
            vmem((2, 4, 8, COLS), F32),
            vmem((2, ROWS, 128), F32),
            vmem((2, ROWS, 128), F32),
            vmem((2, 2, 8, 128), F32),
            vmem((LEVELS, ROWS, COLS), F32),
            vmem((LEVELS, ROWS, HALF), F32),
            vmem((LEVELS, ROWS, HALF), F32),
            vmem((2, LEVELS, 8, HALF), F32),
            vmem((2, LEVELS, 8, HALF), F32),
            vmem((2, LEVELS, 8, HALF // 2), F32),
            vmem((2, LEVELS, 8, HALF), F32),
            vmem((2, LEVELS, 8, HALF), F32),
            vmem((LEVELS, 8, HALF), F32),
            vmem((LEVELS, 8, HALF), F32),
            dma((5,)),
            dma((8,)), dma((8,)),
            dma((LEVELS,)), dma((LEVELS,)),
            dma((6, LEVELS)), dma((6, LEVELS)),
            dma((2, LEVELS)), dma((2, LEVELS)),
            dma((LEVELS,)), dma((LEVELS,)),
            dma((8, LEVELS)), dma((8, LEVELS)),
            dma((4, LEVELS)),
            dma((8, LEVELS)), dma((8, LEVELS)),
        ],
        compiler_params=pltpu.CompilerParams(collective_id=0, has_side_effects=True),
    )(increment, members, zonal_diff, merid_diff, sea_mask)


def solution(mesh):
    return jax.shard_map(
        shards,
        mesh=mesh,
        in_specs=(
            P(None, "gy", "gx"),
            P("mem", None, "gy", "gx"),
            P("gy", "gx"),
            P("gy", "gx"),
            P("gy", "gx"),
        ),
        out_specs=P(None, "gy", "gx"),
        check_vma=False,
    )
```

```python
import jax
import jax.numpy as jnp
from jax import lax
from jax.experimental import pallas as pl
from jax.experimental.pallas import tpu as pltpu
from jax.sharding import PartitionSpec as P

STEPS = 4
LEVELS = 4
ROWS = 64
COLS = 1024
XROWS = ROWS + 8
XCOLS = COLS + 128
HALF = COLS // 2
EAGER = 0
SOON = 2
MESH = pl.DeviceIdType.MESH
F32 = jnp.float32


def kernel(
    inc_hbm, mem_hbm, zon_hbm, mer_hbm, sea_hbm, out,
    inc, mem, zon, mer, sea,
    field, other, edge_cols, edge_rows, wet, east, west, north, south,
    rows_out, rows_in, cols_out, cols_in, corner_in,
    term, peer, part, near, far, split, joint, joined, mine, across,
    load_sem, halo_send, halo_recv, core_send, core_recv,
    red_send, red_recv, join_send, join_recv, y_send, y_recv, ag_send, ag_recv, relay_send, fwd_send, fwd_recv,
):
    me = lax.axis_index("mem")
    gy = lax.axis_index("gy")
    gx = lax.axis_index("gx")
    z = me // 4
    hi = lax.rem(me // 2, 2)
    core = lax.rem(me, 2)

    def member_at(z_, hi_, core_):
        return z_ * 4 + hi_ * 2 + core_

    def beside(dy, dx):
        y = lax.rem(hi * 4 + gy + dy + 8, 8)
        return (member_at(z, y // 4, core), lax.rem(y, 4), lax.rem(gx + dx + 4, 4))

    def along(k):
        return (member_at(lax.rem(z + k + 8, 8), hi, core), gy, gx)

    core_peer = (member_at(z, hi, 1 - core), gy, gx)
    y_peer = (member_at(z, 1 - hi, core), gy, gx)

    barrier = pltpu.get_barrier_semaphore()
    around = [(-1, 0), (1, 0), (0, -1), (0, 1), (-1, -1), (1, -1), (-1, 1), (1, 1)]
    partners = [beside(dy, dx) for dy, dx in around]
    partners += [core_peer, y_peer] + [along(k) for k in range(1, 8)]
    for device in partners:
        pl.semaphore_signal(barrier, inc=1, device_id=device, device_id_type=MESH)

    loads = [
        pltpu.make_async_copy(sea_hbm, sea, load_sem.at[0]),
        pltpu.make_async_copy(zon_hbm, zon, load_sem.at[1]),
        pltpu.make_async_copy(mer_hbm, mer, load_sem.at[2]),
        pltpu.make_async_copy(inc_hbm, inc, load_sem.at[3]),
        pltpu.make_async_copy(mem_hbm.at[0], mem, load_sem.at[4]),
    ]
    for load in loads:
        load.start()
    for load in loads:
        load.wait()

    sub = lax.broadcasted_iota(jnp.int32, (8, 1), 0)
    low = sub < 4
    lane = lax.broadcasted_iota(jnp.int32, (1, 128), 1)

    def start_tile(r, carry):
        at = pl.ds(pl.multiple_of(r * 8, 8), 8)
        m = sea[at, :].astype(F32)
        wet[at, pl.ds(0, COLS)] = m
        for l in range(LEVELS):
            field[l, at, pl.ds(0, COLS)] = mem[l, at, :] * inc[l, at, :] * m
        first = jnp.zeros((8, 128), F32)
        last = jnp.zeros((8, 128), F32)
        left = [field[l, at, pl.ds(0, 128)] for l in range(LEVELS)]
        left += [zon[at, pl.ds(0, 128)], mer[at, pl.ds(0, 128)], m[:, :128]]
        right = [field[l, at, pl.ds(COLS - 128, 128)] for l in range(LEVELS)]
        right += [zon[at, pl.ds(COLS - 128, 128)], mer[at, pl.ds(COLS - 128, 128)], m[:, COLS - 128:]]
        for f in range(7):
            here = (lane >= 4 * f) & (lane < 4 * f + 4)
            a = left[f] if f == 0 else pltpu.roll(left[f], 4 * f, 1)
            b = pltpu.roll(right[f], 4 * f + 4, 1)
            first = jnp.where(here, a, first)
            last = jnp.where(here, b, last)
        cols_out[0, at, :] = first
        cols_out[1, at, :] = last
        return carry

    lax.fori_loop(0, 8, start_tile, 0, unroll=True)

    def tables(at):
        both = [field[l, at, pl.ds(0, COLS)] for l in range(LEVELS)]
        return both + [zon[at, :], mer[at, :], wet[at, pl.ds(0, COLS)]]

    top = tables(pl.ds(0, 8))
    bottom = tables(pl.ds(ROWS - 8, 8))
    for i in range(4):
        if i < 3:
            rows_out[0, i] = jnp.where(low, top[2 * i], pltpu.roll(top[2 * i + 1], 4, 0))
            rows_out[1, i] = jnp.where(low, pltpu.roll(bottom[2 * i + 1], 4, 0), bottom[2 * i])
        else:
            rows_out[0, i] = top[6]
            rows_out[1, i] = bottom[6]

    pl.semaphore_wait(barrier, len(partners))

    def push(src, dst, send, recv, device):
        return pltpu.make_async_remote_copy(
            src_ref=src, dst_ref=dst, send_sem=send, recv_sem=recv,
            device_id=device, device_id_type=MESH,
        )

    halo = [
        push(rows_out.at[0], rows_in.at[0], halo_send.at[0], halo_recv.at[0], beside(-1, 0)),
        push(rows_out.at[1], rows_in.at[1], halo_send.at[1], halo_recv.at[1], beside(1, 0)),
        push(cols_out.at[0], cols_in.at[0], halo_send.at[2], halo_recv.at[2], beside(0, -1)),
        push(cols_out.at[1], cols_in.at[1], halo_send.at[3], halo_recv.at[3], beside(0, 1)),
    ]
    for side in range(2):
        for end in range(2):
            i = side * 2 + end
            halo.append(
                push(
                    cols_out.at[side, pl.ds(end * (ROWS - 8), 8)],
                    corner_in.at[side, end],
                    halo_send.at[4 + i], halo_recv.at[4 + i],
                    beside(-1 if end == 0 else 1, -1 if side == 0 else 1),
                )
            )
    for copy in halo[::-1]:
        copy.start()
    wide = lax.broadcasted_iota(jnp.int32, (1, XCOLS), 1)

    def tile(r):
        return pl.ds(8 * r, 8)

    def shift_up(here, following):
        return jnp.where(sub == 7, pltpu.roll(following, 7, 0), pltpu.roll(here, 7, 0))

    def shift_down(here, preceding):
        return jnp.where(sub == 0, pltpu.roll(preceding, 1, 0), pltpu.roll(here, 1, 0))

    def stepped(u, above, below, weights):
        n = u.shape[1]
        to_east, to_west, to_north, to_south = weights
        go_east = to_east * (pltpu.roll(u, n - 1, 1) - u)
        go_west = to_west * (u - pltpu.roll(u, 1, 1))
        go_north = to_north * (shift_up(u, above) - u)
        go_south = to_south * (u - shift_down(u, below))
        return u + go_east - go_west + go_north - go_south

    own = pl.ds(0, COLS)
    for r in range(8):
        at = tile(r)
        m = wet[at, own]
        weight = zon[at, :] * m * pltpu.roll(m, COLS - 1, 1)
        east[at, own] = weight
        west[at, own] = pltpu.roll(weight, 1, 1)
        north[at, own] = mer[at, :] * m * shift_up(m, wet[tile((r + 1) % 8), own])
    for r in range(8):
        south[tile(r), own] = shift_down(north[tile(r), own], north[tile((r + 7) % 8), own])

    def alone(l, carry):
        for step in range(STEPS):
            src = field.at[l, :, own] if step == 0 else other.at[(step - 1) % 2, :, own]
            dst = other.at[step % 2, :, own]
            for r in range(8):
                at = tile(r)
                weights = [w[at, own] for w in (east, west, north, south)]
                new = stepped(src[at, :], src[tile((r + 1) % 8), :], src[tile((r + 7) % 8), :], weights)
                if step == STEPS - 1:
                    term[l, at, :] = mem[l, at, :] * new
                else:
                    dst[at, :] = new
        return carry

    lax.fori_loop(0, LEVELS, alone, 0)

    for copy in halo:
        copy.wait_recv()

    has_after = gy < 3
    has_before = gy > 0
    edge_ok = jnp.where(low, has_after.astype(jnp.int32), has_before.astype(jnp.int32)) > 0

    after_before = []
    for i in range(4):
        n, s = rows_in[0, i], rows_in[1, i]
        after_before.append(jnp.where(edge_ok, jnp.where(low, n, s), 0.0))
        if i < 3:
            swap = pltpu.roll(jnp.where(low, s, n), 4, 0)
            after_before.append(jnp.where(edge_ok, swap, 0.0))
    tail = pl.ds(ROWS, 8)
    for l in range(LEVELS):
        field[l, tail, pl.ds(0, COLS)] = after_before[l]
    wet[tail, pl.ds(0, COLS)] = after_before[6]

    def side_tile(f, right, left):
        a = right if f == 0 else pltpu.roll(right, 128 - 4 * f, 1)
        b = pltpu.roll(left, 124 - 4 * f, 1)
        return jnp.where(lane < 4, a, jnp.where(lane >= 124, b, 0.0))

    def columns(r, carry):
        at = pl.ds(pl.multiple_of(r * 8, 8), 8)
        right, left = cols_in[0, at, :], cols_in[1, at, :]
        for l in range(LEVELS):
            field[l, at, pl.ds(COLS, 128)] = side_tile(l, right, left)
        east[at, pl.ds(COLS, 128)] = side_tile(4, right, left)
        north[at, pl.ds(COLS, 128)] = side_tile(5, right, left)
        wet[at, pl.ds(COLS, 128)] = side_tile(6, right, left)
        return carry

    lax.fori_loop(0, 8, columns, 0, unroll=True)
    right = jnp.where(edge_ok, jnp.where(low, corner_in[0, 0], corner_in[0, 1]), 0.0)
    left = jnp.where(edge_ok, jnp.where(low, corner_in[1, 0], corner_in[1, 1]), 0.0)
    for l in range(LEVELS):
        field[l, tail, pl.ds(COLS, 128)] = side_tile(l, right, left)
    east[tail, pl.ds(COLS, 128)] = side_tile(4, right, left)
    north[tail, pl.ds(COLS, 128)] = side_tile(5, right, left)
    wet[tail, pl.ds(COLS, 128)] = side_tile(6, right, left)
    east[tail, pl.ds(0, COLS)] = after_before[4]
    north[tail, pl.ds(0, COLS)] = after_before[5]

    inside = (wide < COLS + 3) | (wide >= XCOLS - 4)
    side = pl.ds(COLS - 128, 256)
    inside3 = jnp.concatenate([inside[:, COLS - 128:], inside[:, :128]], axis=1)

    def ring(ref, at):
        return jnp.concatenate([ref[at, side], ref[at, pl.ds(0, 128)]], axis=1)

    for r in range(8):
        at = tile(r)
        m = ring(wet, at)
        z3 = jnp.concatenate([zon[at, pl.ds(COLS - 128, 128)], east[at, pl.ds(COLS, 128)], zon[at, pl.ds(0, 128)]], axis=1)
        weight = jnp.where(inside3, z3 * m * pltpu.roll(m, 383, 1), 0.0)
        east[at, side] = weight[:, :256]
        back = pltpu.roll(weight, 1, 1)
        west[at, pl.ds(COLS, 128)] = back[:, 128:256]
        west[at, pl.ds(0, 128)] = back[:, 256:]
    m = wet[tail, :]
    weight = jnp.where(inside, east[tail, :] * m * pltpu.roll(m, XCOLS - 1, 1), 0.0)
    east[tail, :] = weight
    west[tail, :] = pltpu.roll(weight, 1, 1)
    halo_cols = pl.ds(COLS, 128)
    for r in range(7):
        up = shift_up(wet[tile(r), halo_cols], wet[tile(r + 1), halo_cols])
        north[tile(r), halo_cols] = north[tile(r), halo_cols] * wet[tile(r), halo_cols] * up
    edge = tile(7)
    merid = jnp.concatenate([mer[edge, :], north[edge, halo_cols]], axis=1)
    north[edge, :] = merid * wet[edge, :] * shift_up(wet[edge, :], m)
    weight = north[tail, :] * m * shift_up(m, wet[tile(0), :])
    north[tail, :] = jnp.where(sub == 3, 0.0, weight)
    for r in range(1, 8):
        south[tile(r), halo_cols] = shift_down(north[tile(r), halo_cols], north[tile(r - 1), halo_cols])
    south[tail, :] = shift_down(north[tail, :], north[edge, :])
    south[tile(0), :] = shift_down(north[tile(0), :], north[tail, :])

    def level(l, carry):
        for step in range(STEPS):
            for r in range(8):
                at = tile(r)
                if step == 0:
                    u, a, b = (ring(field.at[l], tile(i % 8)) for i in (r, r + 1, r + 7))
                else:
                    src = edge_cols.at[(step - 1) % 2]
                    u, a, b = (src[tile(i % 8), :] for i in (r, r + 1, r + 7))
                new = stepped(u, a, b, [ring(w, at) for w in (east, west, north, south)])
                if step < STEPS - 1:
                    edge_cols[step % 2, at, :] = new
                    continue
                for lanes, part_, here in ((pl.ds(COLS - 128, 128), new[:, :128], lane >= 124), (pl.ds(0, 128), new[:, 256:], lane < 4)):
                    term[l, at, lanes] = jnp.where(here, mem[l, at, lanes] * part_, term[l, at, lanes])
        order = (7, 8, 0)
        for step in range(STEPS):
            for i, r in enumerate(order):
                if step == STEPS - 1 and r == 8:
                    continue
                if step == 0:
                    u, a, b = (field[l, tile(order[k % 3]), :] for k in (i, i + 1, i + 2))
                else:
                    src = edge_rows.at[(step - 1) % 2]
                    u, a, b = (src[tile(k % 3), :] for k in (i, i + 1, i + 2))
                new = stepped(u, a, b, [w[tile(r), :] for w in (east, west, north, south)])
                if step < STEPS - 1:
                    edge_rows[step % 2, tile(i), :] = new
                    continue
                at = tile(r)
                here = low if r == 0 else jnp.logical_not(low)
                term[l, at, :] = jnp.where(here, mem[l, at, :] * new[:, :COLS], term[l, at, :])
        return carry

    my_half = pl.ds(pl.multiple_of(core * HALF, HALF), HALF)
    their_half = pl.ds(pl.multiple_of((1 - core) * HALF, HALF), HALF)
    my_rows = pl.ds(pl.multiple_of(z * 8, 8), 8)

    def core_copy(l):
        return push(term.at[l, :, their_half], peer.at[l], core_send.at[l], core_recv.at[l], core_peer)

    def rows_of(k):
        return pl.ds(pl.multiple_of(lax.rem(z + k + 8, 8) * 8, 8), 8)

    def first_copies(l):
        copies = []
        for side, sign in enumerate((1, -1)):
            cut = pl.ds(side * (HALF // 2), HALF // 2)
            for i, (src, dst, to) in enumerate((
                (part.at[l, rows_of(3 * sign)], far.at[side, l], sign),
                (part.at[l, rows_of(4), cut], split.at[side, l], 2 * sign),
                (part.at[l, rows_of(sign)], near.at[side, l], sign),
            )):
                at = side * 3 + i
                copies.append(push(src, dst, red_send.at[at, l], red_recv.at[at, l], along(to)))
        return copies

    def second_copies(l):
        return [
            push(joint.at[side, l], joined.at[side, l], join_send.at[side, l], join_recv.at[side, l], along(2 * sign))
            for side, sign in enumerate((1, -1))
        ]

    def y_copy(l):
        return push(mine.at[l], across.at[l], y_send.at[l], y_recv.at[l], y_peer)

    QUARTER = HALF // 2

    def piece_of(l, source, part_):
        start = core * HALF
        if part_ is None:
            where = pl.ds(pl.multiple_of(start, HALF), HALF)
        else:
            where = pl.ds(pl.multiple_of(start + part_ * QUARTER, QUARTER), QUARTER)
        rows = pl.ds(pl.multiple_of(source * 8, 8), 8)
        return out.at[l, rows, where]

    def gather_copies(l, k):
        if k == 4:
            slots = [(3, 0), (7, 1)]
        else:
            slots = [(k - 1, None)]
        copies = []
        for slot, part_ in slots:
            piece = piece_of(l, z, part_)
            copies.append(push(piece, piece, ag_send.at[slot, l], ag_recv.at[slot, l], along(k)))
        return copies

    def soon(k):
        return lax.rem(z + k + 8, 8) < SOON

    def each_owned(l, act, early, late):
        for k in range(1, 8):
            def run(k=k):
                for copy in gather_copies(l, k):
                    act(copy)

            if early:
                pl.when(soon(k))(run)
            if late and k in (1, 2, 6, 7):
                pl.when(jnp.logical_not(soon(k)))(run)

    def relay_copies(l, side):
        sign = 1 - 2 * side
        source = lax.rem(z - 2 * sign + 8, 8)
        whole = piece_of(l, source, None)
        half = piece_of(l, source, side)
        slot = 2 if side == 0 else 4
        half_slot = 3 if side == 0 else 7
        return [
            (sign, push(whole, whole, relay_send.at[2 * side, l], ag_recv.at[slot, l], along(sign))),
            (2 * sign, push(half, half, relay_send.at[2 * side + 1, l], ag_recv.at[half_slot, l], along(2 * sign))),
        ]

    def each_relay(l, side, act):
        for to, copy in relay_copies(l, side):
            @pl.when(jnp.logical_not(soon(to)))
            def _(copy=copy):
                act(copy)

    def arrived(l, k):
        for copy in gather_copies(l, k):
            copy.wait_recv()

    def forward_copy(l, k):
        source = lax.rem(z + 8 - k, 8)
        piece = out.at[l, pl.ds(pl.multiple_of(source * 8, 8), 8), my_half]
        return push(piece, piece, fwd_send.at[k, l], fwd_recv.at[k, l], core_peer)

    def reduce_level(l):
        core_copy(l).wait_recv()
        part[l] = term[l, :, my_half] + peer[l]
        first = first_copies(l)
        for i in (0, 3, 1, 4):
            first[i].start()

    def compute(l, carry):
        level(l, 0)
        core_copy(l).start()

        @pl.when(l > 0)
        def _():
            reduce_level(l - 1)

        return carry

    lax.fori_loop(0, LEVELS, compute, 0)
    reduce_level(LEVELS - 1)

    def join_level(l, carry):
        first = first_copies(l)
        second = second_copies(l)
        for side, sign in enumerate((1, -1)):
            first[side * 3].wait_recv()
            first[side * 3 + 1].wait_recv()
            joint[side, l] = part[l, rows_of(2 * sign), :] + far[side, l]
            cut = pl.ds(side * (HALF // 2), HALF // 2)
            joint[side, l, :, cut] = joint[side, l, :, cut] + split[side, l]
            second[side].start()
        for side in range(2):
            first[side * 3 + 2].start()
        return carry

    lax.fori_loop(0, LEVELS, join_level, 0)

    def sum_level(l, carry):
        first = first_copies(l)
        second = second_copies(l)
        for side in range(2):
            first[side * 3 + 2].wait_recv()
            second[side].wait_recv()
        total = part[l, my_rows, :] + near[0, l] + near[1, l]
        mine[l] = total + joined[0, l] + joined[1, l]
        y_copy(l).start()
        return carry

    lax.fori_loop(0, LEVELS, sum_level, 0)

    def share_level(l, carry):
        y_copy(l).wait_recv()
        out[l, my_rows, my_half] = mine[l] + across[l]
        each_owned(l, lambda copy: copy.start(), True, False)
        forward_copy(l, 0).start()

        @pl.when(l < EAGER)
        def _():
            each_owned(l, lambda copy: copy.start(), False, True)

        return carry

    def later_level(l, carry):
        each_owned(l, lambda copy: copy.start(), False, True)
        return carry

    lax.fori_loop(0, LEVELS, share_level, 0)
    lax.fori_loop(EAGER, LEVELS, later_level, 0)

    def pass_level(l, carry):
        for side, k in enumerate((2, 6)):
            arrived(l, k)
            each_relay(l, side, lambda copy: copy.start())
            forward_copy(l, k).start()
        for k in (1, 7):
            arrived(l, k)
            forward_copy(l, k).start()
        return carry

    def far_level(l, carry):
        for k in (3, 5, 4):
            arrived(l, k)
            forward_copy(l, k).start()
        return carry

    lax.fori_loop(0, LEVELS, pass_level, 0)
    lax.fori_loop(0, LEVELS, far_level, 0)

    def drain(l, carry):
        for k in range(8):
            forward_copy(l, k).wait()
        each_owned(l, lambda copy: copy.wait_send(), True, True)
        for side in range(2):
            each_relay(l, side, lambda copy: copy.wait_send())
        for copy in first_copies(l) + second_copies(l):
            copy.wait_send()
        core_copy(l).wait_send()
        y_copy(l).wait_send()
        return carry

    lax.fori_loop(0, LEVELS, drain, 0)
    for copy in halo:
        copy.wait_send()


def shards(increment, members, zonal_diff, merid_diff, sea_mask):
    vmem = pltpu.VMEM
    dma = pltpu.SemaphoreType.DMA
    return pl.pallas_call(
        kernel,
        out_shape=pltpu.VMEM((LEVELS, ROWS, COLS), F32),
        in_specs=[pl.BlockSpec(memory_space=pl.ANY)] * 5,
        out_specs=pl.BlockSpec(memory_space=pltpu.VMEM),
        scratch_shapes=[
            vmem((LEVELS, ROWS, COLS), F32),
            vmem((LEVELS, ROWS, COLS), F32),
            vmem((ROWS, COLS), F32),
            vmem((ROWS, COLS), F32),
            vmem((ROWS, COLS), jnp.int32),
            vmem((LEVELS, XROWS, XCOLS), F32),
            vmem((2, ROWS, COLS), F32),
            vmem((2, ROWS, 384), F32),
            vmem((2, 24, XCOLS), F32),
            vmem((XROWS, XCOLS), F32),
            vmem((XROWS, XCOLS), F32),
            vmem((XROWS, XCOLS), F32),
            vmem((XROWS, XCOLS), F32),
            vmem((XROWS, XCOLS), F32),
            vmem((2, 4, 8, COLS), F32),
            vmem((2, 4, 8, COLS), F32),
            vmem((2, ROWS, 128), F32),
            vmem((2, ROWS, 128), F32),
            vmem((2, 2, 8, 128), F32),
            vmem((LEVELS, ROWS, COLS), F32),
            vmem((LEVELS, ROWS, HALF), F32),
            vmem((LEVELS, ROWS, HALF), F32),
            vmem((2, LEVELS, 8, HALF), F32),
            vmem((2, LEVELS, 8, HALF), F32),
            vmem((2, LEVELS, 8, HALF // 2), F32),
            vmem((2, LEVELS, 8, HALF), F32),
            vmem((2, LEVELS, 8, HALF), F32),
            vmem((LEVELS, 8, HALF), F32),
            vmem((LEVELS, 8, HALF), F32),
            dma((5,)),
            dma((8,)), dma((8,)),
            dma((LEVELS,)), dma((LEVELS,)),
            dma((6, LEVELS)), dma((6, LEVELS)),
            dma((2, LEVELS)), dma((2, LEVELS)),
            dma((LEVELS,)), dma((LEVELS,)),
            dma((8, LEVELS)), dma((8, LEVELS)),
            dma((4, LEVELS)),
            dma((8, LEVELS)), dma((8, LEVELS)),
        ],
        compiler_params=pltpu.CompilerParams(collective_id=0, has_side_effects=True),
    )(increment, members, zonal_diff, merid_diff, sea_mask)


def solution(mesh):
    return jax.shard_map(
        shards,
        mesh=mesh,
        in_specs=(
            P(None, "gy", "gx"),
            P("mem", None, "gy", "gx"),
            P("gy", "gx"),
            P("gy", "gx"),
            P("gy", "gx"),
        ),
        out_specs=P(None, "gy", "gx"),
        check_vma=False,
    )
```

```python
import jax
import jax.numpy as jnp
from jax import lax
from jax.experimental import pallas as pl
from jax.experimental.pallas import tpu as pltpu
from jax.sharding import PartitionSpec as P

STEPS = 4
LEVELS = 4
ROWS = 64
COLS = 1024
XROWS = ROWS + 8
XCOLS = COLS + 128
HALF = COLS // 2
EAGER = 0
SOON = 2
MESH = pl.DeviceIdType.MESH
F32 = jnp.float32


def kernel(
    inc_hbm, mem_hbm, zon_hbm, mer_hbm, sea_hbm, out,
    inc, mem, zon, mer, sea,
    field, other, edge_cols, edge_rows, wet, east, west, north, south,
    rows_out, rows_in, cols_out, cols_in, corner_in,
    term, peer, part, near, far, split, joint, joined, mine, across,
    load_sem, halo_send, halo_recv, core_send, core_recv,
    red_send, red_recv, join_send, join_recv, y_send, y_recv, ag_send, ag_recv, relay_send, fwd_send, fwd_recv,
):
    me = lax.axis_index("mem")
    gy = lax.axis_index("gy")
    gx = lax.axis_index("gx")
    z = me // 4
    hi = lax.rem(me // 2, 2)
    core = lax.rem(me, 2)

    def member_at(z_, hi_, core_):
        return z_ * 4 + hi_ * 2 + core_

    def beside(dy, dx):
        y = lax.rem(hi * 4 + gy + dy + 8, 8)
        return (member_at(z, y // 4, core), lax.rem(y, 4), lax.rem(gx + dx + 4, 4))

    def along(k):
        return (member_at(lax.rem(z + k + 8, 8), hi, core), gy, gx)

    core_peer = (member_at(z, hi, 1 - core), gy, gx)
    y_peer = (member_at(z, 1 - hi, core), gy, gx)

    barrier = pltpu.get_barrier_semaphore()
    around = [(-1, 0), (1, 0), (0, -1), (0, 1), (-1, -1), (1, -1), (-1, 1), (1, 1)]
    partners = [beside(dy, dx) for dy, dx in around]
    partners += [core_peer, y_peer] + [along(k) for k in range(1, 8)]
    for device in partners:
        pl.semaphore_signal(barrier, inc=1, device_id=device, device_id_type=MESH)

    loads = [
        pltpu.make_async_copy(sea_hbm, sea, load_sem.at[0]),
        pltpu.make_async_copy(zon_hbm, zon, load_sem.at[1]),
        pltpu.make_async_copy(mer_hbm, mer, load_sem.at[2]),
        pltpu.make_async_copy(inc_hbm, inc, load_sem.at[3]),
        pltpu.make_async_copy(mem_hbm.at[0], mem, load_sem.at[4]),
    ]
    for load in loads:
        load.start()
    for load in loads:
        load.wait()

    sub = lax.broadcasted_iota(jnp.int32, (8, 1), 0)
    low = sub < 4
    lane = lax.broadcasted_iota(jnp.int32, (1, 128), 1)

    def start_tile(r, carry):
        at = pl.ds(pl.multiple_of(r * 8, 8), 8)
        m = sea[at, :].astype(F32)
        wet[at, pl.ds(0, COLS)] = m
        for l in range(LEVELS):
            field[l, at, pl.ds(0, COLS)] = mem[l, at, :] * inc[l, at, :] * m
        first = jnp.zeros((8, 128), F32)
        last = jnp.zeros((8, 128), F32)
        left = [field[l, at, pl.ds(0, 128)] for l in range(LEVELS)]
        left += [zon[at, pl.ds(0, 128)], mer[at, pl.ds(0, 128)], m[:, :128]]
        right = [field[l, at, pl.ds(COLS - 128, 128)] for l in range(LEVELS)]
        right += [zon[at, pl.ds(COLS - 128, 128)], mer[at, pl.ds(COLS - 128, 128)], m[:, COLS - 128:]]
        for f in range(7):
            here = (lane >= 4 * f) & (lane < 4 * f + 4)
            a = left[f] if f == 0 else pltpu.roll(left[f], 4 * f, 1)
            b = pltpu.roll(right[f], 4 * f + 4, 1)
            first = jnp.where(here, a, first)
            last = jnp.where(here, b, last)
        cols_out[0, at, :] = first
        cols_out[1, at, :] = last
        return carry

    lax.fori_loop(0, 8, start_tile, 0, unroll=True)

    def tables(at):
        both = [field[l, at, pl.ds(0, COLS)] for l in range(LEVELS)]
        return both + [zon[at, :], mer[at, :], wet[at, pl.ds(0, COLS)]]

    top = tables(pl.ds(0, 8))
    bottom = tables(pl.ds(ROWS - 8, 8))
    for i in range(4):
        if i < 3:
            rows_out[0, i] = jnp.where(low, top[2 * i], pltpu.roll(top[2 * i + 1], 4, 0))
            rows_out[1, i] = jnp.where(low, pltpu.roll(bottom[2 * i + 1], 4, 0), bottom[2 * i])
        else:
            rows_out[0, i] = top[6]
            rows_out[1, i] = bottom[6]

    pl.semaphore_wait(barrier, len(partners))

    def push(src, dst, send, recv, device):
        return pltpu.make_async_remote_copy(
            src_ref=src, dst_ref=dst, send_sem=send, recv_sem=recv,
            device_id=device, device_id_type=MESH,
        )

    halo = [
        push(rows_out.at[0], rows_in.at[0], halo_send.at[0], halo_recv.at[0], beside(-1, 0)),
        push(rows_out.at[1], rows_in.at[1], halo_send.at[1], halo_recv.at[1], beside(1, 0)),
        push(cols_out.at[0], cols_in.at[0], halo_send.at[2], halo_recv.at[2], beside(0, -1)),
        push(cols_out.at[1], cols_in.at[1], halo_send.at[3], halo_recv.at[3], beside(0, 1)),
    ]
    for side in range(2):
        for end in range(2):
            i = side * 2 + end
            halo.append(
                push(
                    cols_out.at[side, pl.ds(end * (ROWS - 8), 8)],
                    corner_in.at[side, end],
                    halo_send.at[4 + i], halo_recv.at[4 + i],
                    beside(-1 if end == 0 else 1, -1 if side == 0 else 1),
                )
            )
    for copy in halo[::-1]:
        copy.start()
    wide = lax.broadcasted_iota(jnp.int32, (1, XCOLS), 1)

    def tile(r):
        return pl.ds(8 * r, 8)

    def shift_up(here, following):
        return jnp.where(sub == 7, pltpu.roll(following, 7, 0), pltpu.roll(here, 7, 0))

    def shift_down(here, preceding):
        return jnp.where(sub == 0, pltpu.roll(preceding, 1, 0), pltpu.roll(here, 1, 0))

    def stepped(u, above, below, weights):
        n = u.shape[1]
        to_east, to_west, to_north, to_south = weights
        go_east = to_east * (pltpu.roll(u, n - 1, 1) - u)
        go_west = to_west * (u - pltpu.roll(u, 1, 1))
        go_north = to_north * (shift_up(u, above) - u)
        go_south = to_south * (u - shift_down(u, below))
        return u + go_east - go_west + go_north - go_south

    own = pl.ds(0, COLS)
    for r in range(8):
        at = tile(r)
        m = wet[at, own]
        weight = zon[at, :] * m * pltpu.roll(m, COLS - 1, 1)
        east[at, own] = weight
        west[at, own] = pltpu.roll(weight, 1, 1)
        north[at, own] = mer[at, :] * m * shift_up(m, wet[tile((r + 1) % 8), own])
    for r in range(8):
        south[tile(r), own] = shift_down(north[tile(r), own], north[tile((r + 7) % 8), own])

    def alone(l, carry):
        for step in range(STEPS):
            src = field.at[l, :, own] if step == 0 else other.at[(step - 1) % 2, :, own]
            dst = other.at[step % 2, :, own]
            for r in range(8):
                at = tile(r)
                weights = [w[at, own] for w in (east, west, north, south)]
                new = stepped(src[at, :], src[tile((r + 1) % 8), :], src[tile((r + 7) % 8), :], weights)
                if step == STEPS - 1:
                    term[l, at, :] = mem[l, at, :] * new
                else:
                    dst[at, :] = new
        return carry

    lax.fori_loop(0, LEVELS, alone, 0)

    for copy in halo:
        copy.wait_recv()

    has_after = gy < 3
    has_before = gy > 0
    edge_ok = jnp.where(low, has_after.astype(jnp.int32), has_before.astype(jnp.int32)) > 0

    after_before = []
    for i in range(4):
        n, s = rows_in[0, i], rows_in[1, i]
        after_before.append(jnp.where(edge_ok, jnp.where(low, n, s), 0.0))
        if i < 3:
            swap = pltpu.roll(jnp.where(low, s, n), 4, 0)
            after_before.append(jnp.where(edge_ok, swap, 0.0))
    tail = pl.ds(ROWS, 8)
    for l in range(LEVELS):
        field[l, tail, pl.ds(0, COLS)] = after_before[l]
    wet[tail, pl.ds(0, COLS)] = after_before[6]

    def side_tile(f, right, left):
        a = right if f == 0 else pltpu.roll(right, 128 - 4 * f, 1)
        b = pltpu.roll(left, 124 - 4 * f, 1)
        return jnp.where(lane < 4, a, jnp.where(lane >= 124, b, 0.0))

    def columns(r, carry):
        at = pl.ds(pl.multiple_of(r * 8, 8), 8)
        right, left = cols_in[0, at, :], cols_in[1, at, :]
        for l in range(LEVELS):
            field[l, at, pl.ds(COLS, 128)] = side_tile(l, right, left)
        east[at, pl.ds(COLS, 128)] = side_tile(4, right, left)
        north[at, pl.ds(COLS, 128)] = side_tile(5, right, left)
        wet[at, pl.ds(COLS, 128)] = side_tile(6, right, left)
        return carry

    lax.fori_loop(0, 8, columns, 0, unroll=True)
    right = jnp.where(edge_ok, jnp.where(low, corner_in[0, 0], corner_in[0, 1]), 0.0)
    left = jnp.where(edge_ok, jnp.where(low, corner_in[1, 0], corner_in[1, 1]), 0.0)
    for l in range(LEVELS):
        field[l, tail, pl.ds(COLS, 128)] = side_tile(l, right, left)
    east[tail, pl.ds(COLS, 128)] = side_tile(4, right, left)
    north[tail, pl.ds(COLS, 128)] = side_tile(5, right, left)
    wet[tail, pl.ds(COLS, 128)] = side_tile(6, right, left)
    east[tail, pl.ds(0, COLS)] = after_before[4]
    north[tail, pl.ds(0, COLS)] = after_before[5]

    inside = (wide < COLS + 3) | (wide >= XCOLS - 4)
    side = pl.ds(COLS - 128, 256)
    inside3 = jnp.concatenate([inside[:, COLS - 128:], inside[:, :128]], axis=1)

    def ring(ref, at):
        return jnp.concatenate([ref[at, side], ref[at, pl.ds(0, 128)]], axis=1)

    for r in range(8):
        at = tile(r)
        m = ring(wet, at)
        z3 = jnp.concatenate([zon[at, pl.ds(COLS - 128, 128)], east[at, pl.ds(COLS, 128)], zon[at, pl.ds(0, 128)]], axis=1)
        weight = jnp.where(inside3, z3 * m * pltpu.roll(m, 383, 1), 0.0)
        east[at, side] = weight[:, :256]
        back = pltpu.roll(weight, 1, 1)
        west[at, pl.ds(COLS, 128)] = back[:, 128:256]
        west[at, pl.ds(0, 128)] = back[:, 256:]
    m = wet[tail, :]
    weight = jnp.where(inside, east[tail, :] * m * pltpu.roll(m, XCOLS - 1, 1), 0.0)
    east[tail, :] = weight
    west[tail, :] = pltpu.roll(weight, 1, 1)
    halo_cols = pl.ds(COLS, 128)
    for r in range(7):
        up = shift_up(wet[tile(r), halo_cols], wet[tile(r + 1), halo_cols])
        north[tile(r), halo_cols] = north[tile(r), halo_cols] * wet[tile(r), halo_cols] * up
    edge = tile(7)
    merid = jnp.concatenate([mer[edge, :], north[edge, halo_cols]], axis=1)
    north[edge, :] = merid * wet[edge, :] * shift_up(wet[edge, :], m)
    weight = north[tail, :] * m * shift_up(m, wet[tile(0), :])
    north[tail, :] = jnp.where(sub == 3, 0.0, weight)
    for r in range(1, 8):
        south[tile(r), halo_cols] = shift_down(north[tile(r), halo_cols], north[tile(r - 1), halo_cols])
    south[tail, :] = shift_down(north[tail, :], north[edge, :])
    south[tile(0), :] = shift_down(north[tile(0), :], north[tail, :])

    def level(l, carry):
        for step in range(STEPS):
            for r in range(8):
                at = tile(r)
                if step == 0:
                    u, a, b = (ring(field.at[l], tile(i % 8)) for i in (r, r + 1, r + 7))
                else:
                    src = edge_cols.at[(step - 1) % 2]
                    u, a, b = (src[tile(i % 8), :] for i in (r, r + 1, r + 7))
                new = stepped(u, a, b, [ring(w, at) for w in (east, west, north, south)])
                if step < STEPS - 1:
                    edge_cols[step % 2, at, :] = new
                    continue
                for lanes, part_, here in ((pl.ds(COLS - 128, 128), new[:, :128], lane >= 124), (pl.ds(0, 128), new[:, 256:], lane < 4)):
                    term[l, at, lanes] = jnp.where(here, mem[l, at, lanes] * part_, term[l, at, lanes])
        order = (7, 8, 0)
        for step in range(STEPS):
            for i, r in enumerate(order):
                if step == STEPS - 1 and r == 8:
                    continue
                if step == 0:
                    u, a, b = (field[l, tile(order[k % 3]), :] for k in (i, i + 1, i + 2))
                else:
                    src = edge_rows.at[(step - 1) % 2]
                    u, a, b = (src[tile(k % 3), :] for k in (i, i + 1, i + 2))
                new = stepped(u, a, b, [w[tile(r), :] for w in (east, west, north, south)])
                if step < STEPS - 1:
                    edge_rows[step % 2, tile(i), :] = new
                    continue
                at = tile(r)
                here = low if r == 0 else jnp.logical_not(low)
                term[l, at, :] = jnp.where(here, mem[l, at, :] * new[:, :COLS], term[l, at, :])
        return carry

    my_half = pl.ds(pl.multiple_of(core * HALF, HALF), HALF)
    their_half = pl.ds(pl.multiple_of((1 - core) * HALF, HALF), HALF)
    my_rows = pl.ds(pl.multiple_of(z * 8, 8), 8)

    def core_copy(l):
        return push(term.at[l, :, their_half], peer.at[l], core_send.at[l], core_recv.at[l], core_peer)

    def rows_of(k):
        return pl.ds(pl.multiple_of(lax.rem(z + k + 8, 8) * 8, 8), 8)

    def first_copies(l):
        copies = []
        for side, sign in enumerate((1, -1)):
            cut = pl.ds(side * (HALF // 2), HALF // 2)
            for i, (src, dst, to) in enumerate((
                (part.at[l, rows_of(3 * sign)], far.at[side, l], sign),
                (part.at[l, rows_of(4), cut], split.at[side, l], 2 * sign),
                (part.at[l, rows_of(sign)], near.at[side, l], sign),
            )):
                at = side * 3 + i
                copies.append(push(src, dst, red_send.at[at, l], red_recv.at[at, l], along(to)))
        return copies

    def second_copies(l):
        return [
            push(joint.at[side, l], joined.at[side, l], join_send.at[side, l], join_recv.at[side, l], along(2 * sign))
            for side, sign in enumerate((1, -1))
        ]

    def y_copy(l):
        return push(mine.at[l], across.at[l], y_send.at[l], y_recv.at[l], y_peer)

    QUARTER = HALF // 2

    def piece_of(l, source, part_):
        start = core * HALF
        if part_ is None:
            where = pl.ds(pl.multiple_of(start, HALF), HALF)
        else:
            where = pl.ds(pl.multiple_of(start + part_ * QUARTER, QUARTER), QUARTER)
        rows = pl.ds(pl.multiple_of(source * 8, 8), 8)
        return out.at[l, rows, where]

    def gather_copies(l, k):
        if k == 4:
            slots = [(3, 0), (7, 1)]
        else:
            slots = [(k - 1, None)]
        copies = []
        for slot, part_ in slots:
            piece = piece_of(l, z, part_)
            copies.append(push(piece, piece, ag_send.at[slot, l], ag_recv.at[slot, l], along(k)))
        return copies

    def soon(k):
        return lax.rem(z + k + 8, 8) < SOON

    def each_owned(l, act, early, late):
        for k in range(1, 8):
            def run(k=k):
                for copy in gather_copies(l, k):
                    act(copy)

            if early:
                pl.when(soon(k))(run)
            if late and k in (1, 2, 6, 7):
                pl.when(jnp.logical_not(soon(k)))(run)

    def relay_copies(l, side):
        sign = 1 - 2 * side
        source = lax.rem(z - 2 * sign + 8, 8)
        whole = piece_of(l, source, None)
        half = piece_of(l, source, side)
        slot = 2 if side == 0 else 4
        half_slot = 3 if side == 0 else 7
        return [
            (sign, push(whole, whole, relay_send.at[2 * side, l], ag_recv.at[slot, l], along(sign))),
            (2 * sign, push(half, half, relay_send.at[2 * side + 1, l], ag_recv.at[half_slot, l], along(2 * sign))),
        ]

    def each_relay(l, side, act):
        for to, copy in relay_copies(l, side):
            @pl.when(jnp.logical_not(soon(to)))
            def _(copy=copy):
                act(copy)

    def arrived(l, k):
        for copy in gather_copies(l, k):
            copy.wait_recv()

    def forward_copy(l, k):
        source = lax.rem(z + 8 - k, 8)
        piece = out.at[l, pl.ds(pl.multiple_of(source * 8, 8), 8), my_half]
        return push(piece, piece, fwd_send.at[k, l], fwd_recv.at[k, l], core_peer)

    def reduce_level(l):
        core_copy(l).wait_recv()
        part[l] = term[l, :, my_half] + peer[l]
        first = first_copies(l)
        for i in (0, 3, 1, 4):
            first[i].start()

    def compute(l, carry):
        level(l, 0)
        core_copy(l).start()

        @pl.when(l > 0)
        def _():
            reduce_level(l - 1)

        return carry

    lax.fori_loop(0, LEVELS, compute, 0)
    reduce_level(LEVELS - 1)

    def join_level(l, carry):
        first = first_copies(l)
        second = second_copies(l)
        for side, sign in enumerate((1, -1)):
            first[side * 3].wait_recv()
            first[side * 3 + 1].wait_recv()
            joint[side, l] = part[l, rows_of(2 * sign), :] + far[side, l]
            cut = pl.ds(side * (HALF // 2), HALF // 2)
            joint[side, l, :, cut] = joint[side, l, :, cut] + split[side, l]
            second[side].start()
        for side in range(2):
            first[side * 3 + 2].start()
        return carry

    lax.fori_loop(0, LEVELS, join_level, 0)

    def sum_level(l, carry):
        first = first_copies(l)
        second = second_copies(l)
        for side in range(2):
            first[side * 3 + 2].wait_recv()
            second[side].wait_recv()
        total = part[l, my_rows, :] + near[0, l] + near[1, l]
        mine[l] = total + joined[0, l] + joined[1, l]
        y_copy(l).start()
        return carry

    lax.fori_loop(0, LEVELS, sum_level, 0)

    def share_level(l, carry):
        y_copy(l).wait_recv()
        out[l, my_rows, my_half] = mine[l] + across[l]
        each_owned(l, lambda copy: copy.start(), True, False)
        forward_copy(l, 0).start()

        @pl.when(l < EAGER)
        def _():
            each_owned(l, lambda copy: copy.start(), False, True)

        return carry

    def later_level(l, carry):
        each_owned(l, lambda copy: copy.start(), False, True)
        return carry

    lax.fori_loop(0, LEVELS, share_level, 0)
    lax.fori_loop(EAGER, LEVELS, later_level, 0)

    def far_pieces(l):
        for k in (3, 5, 4):
            arrived(l, k)
            forward_copy(l, k).start()

    def far_level(l, carry):
        pl.when(z >= SOON)(lambda: far_pieces(l))
        return carry

    def pass_level(l, carry):
        for side, k in enumerate((2, 6)):
            arrived(l, k)
            each_relay(l, side, lambda copy: copy.start())
            forward_copy(l, k).start()
        for k in (1, 7):
            arrived(l, k)
            forward_copy(l, k).start()
        pl.when(z < SOON)(lambda: far_pieces(l))
        return carry

    lax.fori_loop(0, LEVELS, pass_level, 0)
    lax.fori_loop(0, LEVELS, far_level, 0)

    def drain(l, carry):
        for k in range(8):
            forward_copy(l, k).wait()
        each_owned(l, lambda copy: copy.wait_send(), True, True)
        for side in range(2):
            each_relay(l, side, lambda copy: copy.wait_send())
        for copy in first_copies(l) + second_copies(l):
            copy.wait_send()
        core_copy(l).wait_send()
        y_copy(l).wait_send()
        return carry

    lax.fori_loop(0, LEVELS, drain, 0)
    for copy in halo:
        copy.wait_send()


def shards(increment, members, zonal_diff, merid_diff, sea_mask):
    vmem = pltpu.VMEM
    dma = pltpu.SemaphoreType.DMA
    return pl.pallas_call(
        kernel,
        out_shape=pltpu.VMEM((LEVELS, ROWS, COLS), F32),
        in_specs=[pl.BlockSpec(memory_space=pl.ANY)] * 5,
        out_specs=pl.BlockSpec(memory_space=pltpu.VMEM),
        scratch_shapes=[
            vmem((LEVELS, ROWS, COLS), F32),
            vmem((LEVELS, ROWS, COLS), F32),
            vmem((ROWS, COLS), F32),
            vmem((ROWS, COLS), F32),
            vmem((ROWS, COLS), jnp.int32),
            vmem((LEVELS, XROWS, XCOLS), F32),
            vmem((2, ROWS, COLS), F32),
            vmem((2, ROWS, 384), F32),
            vmem((2, 24, XCOLS), F32),
            vmem((XROWS, XCOLS), F32),
            vmem((XROWS, XCOLS), F32),
            vmem((XROWS, XCOLS), F32),
            vmem((XROWS, XCOLS), F32),
            vmem((XROWS, XCOLS), F32),
            vmem((2, 4, 8, COLS), F32),
            vmem((2, 4, 8, COLS), F32),
            vmem((2, ROWS, 128), F32),
            vmem((2, ROWS, 128), F32),
            vmem((2, 2, 8, 128), F32),
            vmem((LEVELS, ROWS, COLS), F32),
            vmem((LEVELS, ROWS, HALF), F32),
            vmem((LEVELS, ROWS, HALF), F32),
            vmem((2, LEVELS, 8, HALF), F32),
            vmem((2, LEVELS, 8, HALF), F32),
            vmem((2, LEVELS, 8, HALF // 2), F32),
            vmem((2, LEVELS, 8, HALF), F32),
            vmem((2, LEVELS, 8, HALF), F32),
            vmem((LEVELS, 8, HALF), F32),
            vmem((LEVELS, 8, HALF), F32),
            dma((5,)),
            dma((8,)), dma((8,)),
            dma((LEVELS,)), dma((LEVELS,)),
            dma((6, LEVELS)), dma((6, LEVELS)),
            dma((2, LEVELS)), dma((2, LEVELS)),
            dma((LEVELS,)), dma((LEVELS,)),
            dma((8, LEVELS)), dma((8, LEVELS)),
            dma((4, LEVELS)),
            dma((8, LEVELS)), dma((8, LEVELS)),
        ],
        compiler_params=pltpu.CompilerParams(collective_id=0, has_side_effects=True),
    )(increment, members, zonal_diff, merid_diff, sea_mask)


def solution(mesh):
    return jax.shard_map(
        shards,
        mesh=mesh,
        in_specs=(
            P(None, "gy", "gx"),
            P("mem", None, "gy", "gx"),
            P("gy", "gx"),
            P("gy", "gx"),
            P("gy", "gx"),
        ),
        out_specs=P(None, "gy", "gx"),
        check_vma=False,
    )
```

```python
import jax
import jax.numpy as jnp
from jax import lax
from jax.experimental import pallas as pl
from jax.experimental.pallas import tpu as pltpu
from jax.sharding import PartitionSpec as P

STEPS = 4
LEVELS = 4
ROWS = 64
COLS = 1024
XROWS = ROWS + 8
XCOLS = COLS + 128
HALF = COLS // 2
EAGER = 0
SOON = 2
MESH = pl.DeviceIdType.MESH
F32 = jnp.float32


def kernel(
    inc_hbm, mem_hbm, zon_hbm, mer_hbm, sea_hbm, out,
    inc, mem, zon, mer, sea,
    field, other, edge_cols, edge_rows, wet, east, west, north, south,
    rows_out, rows_in, cols_out, cols_in, corner_in,
    term, peer, part, near, far, split, joint, joined, mine, across,
    load_sem, halo_send, halo_recv, core_send, core_recv,
    red_send, red_recv, join_send, join_recv, y_send, y_recv, ag_send, ag_recv, relay_send, fwd_send, fwd_recv,
):
    me = lax.axis_index("mem")
    gy = lax.axis_index("gy")
    gx = lax.axis_index("gx")
    z = me // 4
    hi = lax.rem(me // 2, 2)
    core = lax.rem(me, 2)

    def member_at(z_, hi_, core_):
        return z_ * 4 + hi_ * 2 + core_

    def beside(dy, dx):
        y = lax.rem(hi * 4 + gy + dy + 8, 8)
        return (member_at(z, y // 4, core), lax.rem(y, 4), lax.rem(gx + dx + 4, 4))

    def along(k):
        return (member_at(lax.rem(z + k + 8, 8), hi, core), gy, gx)

    core_peer = (member_at(z, hi, 1 - core), gy, gx)
    y_peer = (member_at(z, 1 - hi, core), gy, gx)

    barrier = pltpu.get_barrier_semaphore()
    around = [(-1, 0), (1, 0), (0, -1), (0, 1), (-1, -1), (1, -1), (-1, 1), (1, 1)]
    partners = [beside(dy, dx) for dy, dx in around]
    partners += [core_peer, y_peer] + [along(k) for k in range(1, 8)]
    for device in partners:
        pl.semaphore_signal(barrier, inc=1, device_id=device, device_id_type=MESH)

    loads = [
        pltpu.make_async_copy(sea_hbm, sea, load_sem.at[0]),
        pltpu.make_async_copy(zon_hbm, zon, load_sem.at[1]),
        pltpu.make_async_copy(mer_hbm, mer, load_sem.at[2]),
        pltpu.make_async_copy(inc_hbm, inc, load_sem.at[3]),
        pltpu.make_async_copy(mem_hbm.at[0], mem, load_sem.at[4]),
    ]
    for load in loads:
        load.start()
    for load in loads:
        load.wait()

    sub = lax.broadcasted_iota(jnp.int32, (8, 1), 0)
    low = sub < 4
    lane = lax.broadcasted_iota(jnp.int32, (1, 128), 1)

    def start_tile(r, carry):
        at = pl.ds(pl.multiple_of(r * 8, 8), 8)
        m = sea[at, :].astype(F32)
        wet[at, pl.ds(0, COLS)] = m
        for l in range(LEVELS):
            field[l, at, pl.ds(0, COLS)] = mem[l, at, :] * inc[l, at, :] * m
        first = jnp.zeros((8, 128), F32)
        last = jnp.zeros((8, 128), F32)
        left = [field[l, at, pl.ds(0, 128)] for l in range(LEVELS)]
        left += [zon[at, pl.ds(0, 128)], mer[at, pl.ds(0, 128)], m[:, :128]]
        right = [field[l, at, pl.ds(COLS - 128, 128)] for l in range(LEVELS)]
        right += [zon[at, pl.ds(COLS - 128, 128)], mer[at, pl.ds(COLS - 128, 128)], m[:, COLS - 128:]]
        for f in range(7):
            here = (lane >= 4 * f) & (lane < 4 * f + 4)
            a = left[f] if f == 0 else pltpu.roll(left[f], 4 * f, 1)
            b = pltpu.roll(right[f], 4 * f + 4, 1)
            first = jnp.where(here, a, first)
            last = jnp.where(here, b, last)
        cols_out[0, at, :] = first
        cols_out[1, at, :] = last
        return carry

    lax.fori_loop(0, 8, start_tile, 0, unroll=True)

    def tables(at):
        both = [field[l, at, pl.ds(0, COLS)] for l in range(LEVELS)]
        return both + [zon[at, :], mer[at, :], wet[at, pl.ds(0, COLS)]]

    top = tables(pl.ds(0, 8))
    bottom = tables(pl.ds(ROWS - 8, 8))
    for i in range(4):
        if i < 3:
            rows_out[0, i] = jnp.where(low, top[2 * i], pltpu.roll(top[2 * i + 1], 4, 0))
            rows_out[1, i] = jnp.where(low, pltpu.roll(bottom[2 * i + 1], 4, 0), bottom[2 * i])
        else:
            rows_out[0, i] = top[6]
            rows_out[1, i] = bottom[6]

    pl.semaphore_wait(barrier, len(partners))

    def push(src, dst, send, recv, device):
        return pltpu.make_async_remote_copy(
            src_ref=src, dst_ref=dst, send_sem=send, recv_sem=recv,
            device_id=device, device_id_type=MESH,
        )

    halo = [
        push(rows_out.at[0], rows_in.at[0], halo_send.at[0], halo_recv.at[0], beside(-1, 0)),
        push(rows_out.at[1], rows_in.at[1], halo_send.at[1], halo_recv.at[1], beside(1, 0)),
        push(cols_out.at[0], cols_in.at[0], halo_send.at[2], halo_recv.at[2], beside(0, -1)),
        push(cols_out.at[1], cols_in.at[1], halo_send.at[3], halo_recv.at[3], beside(0, 1)),
    ]
    for side in range(2):
        for end in range(2):
            i = side * 2 + end
            halo.append(
                push(
                    cols_out.at[side, pl.ds(end * (ROWS - 8), 8)],
                    corner_in.at[side, end],
                    halo_send.at[4 + i], halo_recv.at[4 + i],
                    beside(-1 if end == 0 else 1, -1 if side == 0 else 1),
                )
            )
    for copy in halo[::-1]:
        copy.start()
    wide = lax.broadcasted_iota(jnp.int32, (1, XCOLS), 1)

    def tile(r):
        return pl.ds(8 * r, 8)

    def shift_up(here, following):
        return jnp.where(sub == 7, pltpu.roll(following, 7, 0), pltpu.roll(here, 7, 0))

    def shift_down(here, preceding):
        return jnp.where(sub == 0, pltpu.roll(preceding, 1, 0), pltpu.roll(here, 1, 0))

    def stepped(u, above, below, weights):
        n = u.shape[1]
        to_east, to_west, to_north, to_south = weights
        go_east = to_east * (pltpu.roll(u, n - 1, 1) - u)
        go_west = to_west * (u - pltpu.roll(u, 1, 1))
        go_north = to_north * (shift_up(u, above) - u)
        go_south = to_south * (u - shift_down(u, below))
        return u + go_east - go_west + go_north - go_south

    own = pl.ds(0, COLS)
    for r in range(8):
        at = tile(r)
        m = wet[at, own]
        weight = zon[at, :] * m * pltpu.roll(m, COLS - 1, 1)
        east[at, own] = weight
        west[at, own] = pltpu.roll(weight, 1, 1)
        north[at, own] = mer[at, :] * m * shift_up(m, wet[tile((r + 1) % 8), own])
    for r in range(8):
        south[tile(r), own] = shift_down(north[tile(r), own], north[tile((r + 7) % 8), own])

    def alone(l, carry):
        for step in range(STEPS):
            src = field.at[l, :, own] if step == 0 else other.at[(step - 1) % 2, :, own]
            dst = other.at[step % 2, :, own]
            for r in range(8):
                at = tile(r)
                weights = [w[at, own] for w in (east, west, north, south)]
                new = stepped(src[at, :], src[tile((r + 1) % 8), :], src[tile((r + 7) % 8), :], weights)
                if step == STEPS - 1:
                    term[l, at, :] = mem[l, at, :] * new
                else:
                    dst[at, :] = new
        return carry

    lax.fori_loop(0, LEVELS, alone, 0)

    for copy in halo[2:4]:
        copy.wait_recv()

    def side_tile(f, right, left):
        a = right if f == 0 else pltpu.roll(right, 128 - 4 * f, 1)
        b = pltpu.roll(left, 124 - 4 * f, 1)
        return jnp.where(lane < 4, a, jnp.where(lane >= 124, b, 0.0))

    halo_cols = pl.ds(COLS, 128)
    for r in range(8):
        at = tile(r)
        right, left = cols_in[0, at, :], cols_in[1, at, :]
        for l in range(LEVELS):
            field[l, at, halo_cols] = side_tile(l, right, left)
        east[at, halo_cols] = side_tile(4, right, left)
        north[at, halo_cols] = side_tile(5, right, left)
        wet[at, halo_cols] = side_tile(6, right, left)

    inside = (wide < COLS + 3) | (wide >= XCOLS - 4)
    side = pl.ds(COLS - 128, 256)
    inside3 = jnp.concatenate([inside[:, COLS - 128:], inside[:, :128]], axis=1)

    def ring(ref, at):
        return jnp.concatenate([ref[at, side], ref[at, pl.ds(0, 128)]], axis=1)

    for r in range(8):
        at = tile(r)
        m = ring(wet, at)
        z3 = jnp.concatenate([zon[at, pl.ds(COLS - 128, 128)], east[at, halo_cols], zon[at, pl.ds(0, 128)]], axis=1)
        weight = jnp.where(inside3, z3 * m * pltpu.roll(m, 383, 1), 0.0)
        east[at, side] = weight[:, :256]
        back = pltpu.roll(weight, 1, 1)
        west[at, halo_cols] = back[:, 128:256]
        west[at, pl.ds(0, 128)] = back[:, 256:]
        up = shift_up(m[:, 128:256], wet[tile((r + 1) % 8), halo_cols])
        north[at, halo_cols] = north[at, halo_cols] * m[:, 128:256] * up
    for r in range(8):
        south[tile(r), halo_cols] = shift_down(north[tile(r), halo_cols], north[tile((r + 7) % 8), halo_cols])

    def near_cols(l, carry):
        for step in range(STEPS):
            for r in range(8):
                at = tile(r)
                if step == 0:
                    u, a, b = (ring(field.at[l], tile(i % 8)) for i in (r, r + 1, r + 7))
                else:
                    src = edge_cols.at[(step - 1) % 2]
                    u, a, b = (src[tile(i % 8), :] for i in (r, r + 1, r + 7))
                new = stepped(u, a, b, [ring(w, at) for w in (east, west, north, south)])
                if step < STEPS - 1:
                    edge_cols[step % 2, at, :] = new
                    continue
                for lanes, part_, here in ((pl.ds(COLS - 128, 128), new[:, :128], lane >= 124), (pl.ds(0, 128), new[:, 256:], lane < 4)):
                    term[l, at, lanes] = jnp.where(here, mem[l, at, lanes] * part_, term[l, at, lanes])
        return carry

    lax.fori_loop(0, LEVELS, near_cols, 0)

    for copy in halo[:2] + halo[4:]:
        copy.wait_recv()

    has_after = gy < 3
    has_before = gy > 0
    edge_ok = jnp.where(low, has_after.astype(jnp.int32), has_before.astype(jnp.int32)) > 0

    after_before = []
    for i in range(4):
        n, s = rows_in[0, i], rows_in[1, i]
        after_before.append(jnp.where(edge_ok, jnp.where(low, n, s), 0.0))
        if i < 3:
            swap = pltpu.roll(jnp.where(low, s, n), 4, 0)
            after_before.append(jnp.where(edge_ok, swap, 0.0))
    tail = pl.ds(ROWS, 8)
    right = jnp.where(edge_ok, jnp.where(low, corner_in[0, 0], corner_in[0, 1]), 0.0)
    left = jnp.where(edge_ok, jnp.where(low, corner_in[1, 0], corner_in[1, 1]), 0.0)
    for l in range(LEVELS):
        field[l, tail, own] = after_before[l]
        field[l, tail, halo_cols] = side_tile(l, right, left)
    zonal = jnp.concatenate([after_before[4], side_tile(4, right, left)], axis=1)
    merid = jnp.concatenate([after_before[5], side_tile(5, right, left)], axis=1)
    m = jnp.concatenate([after_before[6], side_tile(6, right, left)], axis=1)
    weight = jnp.where(inside, zonal * m * pltpu.roll(m, XCOLS - 1, 1), 0.0)
    east[tail, :] = weight
    west[tail, :] = pltpu.roll(weight, 1, 1)
    edge = tile(7)
    edge_side = side_tile(5, cols_in[0, edge, :], cols_in[1, edge, :])
    edge_merid = jnp.concatenate([mer[edge, :], edge_side], axis=1)
    last = edge_merid * wet[edge, :] * shift_up(wet[edge, :], m)
    north[edge, :] = last
    beyond = jnp.where(sub == 3, 0.0, merid * m * shift_up(m, wet[tile(0), :]))
    north[tail, :] = beyond
    south[tail, :] = shift_down(beyond, last)
    south[tile(0), :] = shift_down(north[tile(0), :], beyond)

    def level(l, carry):
        order = (7, 8, 0)
        for step in range(STEPS):
            for i, r in enumerate(order):
                if step == STEPS - 1 and r == 8:
                    continue
                if step == 0:
                    u, a, b = (field[l, tile(order[k % 3]), :] for k in (i, i + 1, i + 2))
                else:
                    src = edge_rows.at[(step - 1) % 2]
                    u, a, b = (src[tile(k % 3), :] for k in (i, i + 1, i + 2))
                new = stepped(u, a, b, [w[tile(r), :] for w in (east, west, north, south)])
                if step < STEPS - 1:
                    edge_rows[step % 2, tile(i), :] = new
                    continue
                at = tile(r)
                here = low if r == 0 else jnp.logical_not(low)
                term[l, at, :] = jnp.where(here, mem[l, at, :] * new[:, :COLS], term[l, at, :])
        return carry

    my_half = pl.ds(pl.multiple_of(core * HALF, HALF), HALF)
    their_half = pl.ds(pl.multiple_of((1 - core) * HALF, HALF), HALF)
    my_rows = pl.ds(pl.multiple_of(z * 8, 8), 8)

    def core_copy(l):
        return push(term.at[l, :, their_half], peer.at[l], core_send.at[l], core_recv.at[l], core_peer)

    def rows_of(k):
        return pl.ds(pl.multiple_of(lax.rem(z + k + 8, 8) * 8, 8), 8)

    def first_copies(l):
        copies = []
        for side, sign in enumerate((1, -1)):
            cut = pl.ds(side * (HALF // 2), HALF // 2)
            for i, (src, dst, to) in enumerate((
                (part.at[l, rows_of(3 * sign)], far.at[side, l], sign),
                (part.at[l, rows_of(4), cut], split.at[side, l], 2 * sign),
                (part.at[l, rows_of(sign)], near.at[side, l], sign),
            )):
                at = side * 3 + i
                copies.append(push(src, dst, red_send.at[at, l], red_recv.at[at, l], along(to)))
        return copies

    def second_copies(l):
        return [
            push(joint.at[side, l], joined.at[side, l], join_send.at[side, l], join_recv.at[side, l], along(2 * sign))
            for side, sign in enumerate((1, -1))
        ]

    def y_copy(l):
        return push(mine.at[l], across.at[l], y_send.at[l], y_recv.at[l], y_peer)

    QUARTER = HALF // 2

    def piece_of(l, source, part_):
        start = core * HALF
        if part_ is None:
            where = pl.ds(pl.multiple_of(start, HALF), HALF)
        else:
            where = pl.ds(pl.multiple_of(start + part_ * QUARTER, QUARTER), QUARTER)
        rows = pl.ds(pl.multiple_of(source * 8, 8), 8)
        return out.at[l, rows, where]

    def gather_copies(l, k):
        if k == 4:
            slots = [(3, 0), (7, 1)]
        else:
            slots = [(k - 1, None)]
        copies = []
        for slot, part_ in slots:
            piece = piece_of(l, z, part_)
            copies.append(push(piece, piece, ag_send.at[slot, l], ag_recv.at[slot, l], along(k)))
        return copies

    def soon(k):
        return lax.rem(z + k + 8, 8) < SOON

    def each_owned(l, act, early, late):
        for k in range(1, 8):
            def run(k=k):
                for copy in gather_copies(l, k):
                    act(copy)

            if early:
                pl.when(soon(k))(run)
            if late and k in (1, 2, 6, 7):
                pl.when(jnp.logical_not(soon(k)))(run)

    def relay_copies(l, side):
        sign = 1 - 2 * side
        source = lax.rem(z - 2 * sign + 8, 8)
        whole = piece_of(l, source, None)
        half = piece_of(l, source, side)
        slot = 2 if side == 0 else 4
        half_slot = 3 if side == 0 else 7
        return [
            (sign, push(whole, whole, relay_send.at[2 * side, l], ag_recv.at[slot, l], along(sign))),
            (2 * sign, push(half, half, relay_send.at[2 * side + 1, l], ag_recv.at[half_slot, l], along(2 * sign))),
        ]

    def each_relay(l, side, act):
        for to, copy in relay_copies(l, side):
            @pl.when(jnp.logical_not(soon(to)))
            def _(copy=copy):
                act(copy)

    def arrived(l, k):
        for copy in gather_copies(l, k):
            copy.wait_recv()

    def forward_copy(l, k):
        source = lax.rem(z + 8 - k, 8)
        piece = out.at[l, pl.ds(pl.multiple_of(source * 8, 8), 8), my_half]
        return push(piece, piece, fwd_send.at[k, l], fwd_recv.at[k, l], core_peer)

    def reduce_level(l):
        core_copy(l).wait_recv()
        part[l] = term[l, :, my_half] + peer[l]
        first = first_copies(l)
        for i in (0, 3, 1, 4):
            first[i].start()

    def compute(l, carry):
        level(l, 0)
        core_copy(l).start()
        return carry

    lax.fori_loop(0, LEVELS, compute, 0)

    def reduce_all(l, carry):
        reduce_level(l)
        return carry

    lax.fori_loop(0, LEVELS, reduce_all, 0)

    def join_level(l, carry):
        first = first_copies(l)
        second = second_copies(l)
        for side, sign in enumerate((1, -1)):
            first[side * 3].wait_recv()
            first[side * 3 + 1].wait_recv()
            joint[side, l] = part[l, rows_of(2 * sign), :] + far[side, l]
            cut = pl.ds(side * (HALF // 2), HALF // 2)
            joint[side, l, :, cut] = joint[side, l, :, cut] + split[side, l]
            second[side].start()
        for side in range(2):
            first[side * 3 + 2].start()
        return carry

    lax.fori_loop(0, LEVELS, join_level, 0)

    def sum_level(l, carry):
        first = first_copies(l)
        second = second_copies(l)
        for side in range(2):
            first[side * 3 + 2].wait_recv()
            second[side].wait_recv()
        total = part[l, my_rows, :] + near[0, l] + near[1, l]
        mine[l] = total + joined[0, l] + joined[1, l]
        y_copy(l).start()
        return carry

    lax.fori_loop(0, LEVELS, sum_level, 0)

    def share_level(l, carry):
        y_copy(l).wait_recv()
        out[l, my_rows, my_half] = mine[l] + across[l]
        each_owned(l, lambda copy: copy.start(), True, False)
        forward_copy(l, 0).start()

        @pl.when(l < EAGER)
        def _():
            each_owned(l, lambda copy: copy.start(), False, True)

        return carry

    def later_level(l, carry):
        each_owned(l, lambda copy: copy.start(), False, True)
        return carry

    lax.fori_loop(0, LEVELS, share_level, 0)
    lax.fori_loop(EAGER, LEVELS, later_level, 0)

    def far_pieces(l):
        for k in (3, 5, 4):
            arrived(l, k)
            forward_copy(l, k).start()

    def far_level(l, carry):
        pl.when(z >= SOON)(lambda: far_pieces(l))
        return carry

    def pass_level(l, carry):
        for side, k in enumerate((2, 6)):
            arrived(l, k)
            each_relay(l, side, lambda copy: copy.start())
            forward_copy(l, k).start()
        for k in (1, 7):
            arrived(l, k)
            forward_copy(l, k).start()
        pl.when(z < SOON)(lambda: far_pieces(l))
        return carry

    lax.fori_loop(0, LEVELS, pass_level, 0)
    lax.fori_loop(0, LEVELS, far_level, 0)

    def drain(l, carry):
        for k in range(8):
            forward_copy(l, k).wait()
        each_owned(l, lambda copy: copy.wait_send(), True, True)
        for side in range(2):
            each_relay(l, side, lambda copy: copy.wait_send())
        for copy in first_copies(l) + second_copies(l):
            copy.wait_send()
        core_copy(l).wait_send()
        y_copy(l).wait_send()
        return carry

    lax.fori_loop(0, LEVELS, drain, 0)
    for copy in halo:
        copy.wait_send()


def shards(increment, members, zonal_diff, merid_diff, sea_mask):
    vmem = pltpu.VMEM
    dma = pltpu.SemaphoreType.DMA
    return pl.pallas_call(
        kernel,
        out_shape=pltpu.VMEM((LEVELS, ROWS, COLS), F32),
        in_specs=[pl.BlockSpec(memory_space=pl.ANY)] * 5,
        out_specs=pl.BlockSpec(memory_space=pltpu.VMEM),
        scratch_shapes=[
            vmem((LEVELS, ROWS, COLS), F32),
            vmem((LEVELS, ROWS, COLS), F32),
            vmem((ROWS, COLS), F32),
            vmem((ROWS, COLS), F32),
            vmem((ROWS, COLS), jnp.int32),
            vmem((LEVELS, XROWS, XCOLS), F32),
            vmem((2, ROWS, COLS), F32),
            vmem((2, ROWS, 384), F32),
            vmem((2, 24, XCOLS), F32),
            vmem((XROWS, XCOLS), F32),
            vmem((XROWS, XCOLS), F32),
            vmem((XROWS, XCOLS), F32),
            vmem((XROWS, XCOLS), F32),
            vmem((XROWS, XCOLS), F32),
            vmem((2, 4, 8, COLS), F32),
            vmem((2, 4, 8, COLS), F32),
            vmem((2, ROWS, 128), F32),
            vmem((2, ROWS, 128), F32),
            vmem((2, 2, 8, 128), F32),
            vmem((LEVELS, ROWS, COLS), F32),
            vmem((LEVELS, ROWS, HALF), F32),
            vmem((LEVELS, ROWS, HALF), F32),
            vmem((2, LEVELS, 8, HALF), F32),
            vmem((2, LEVELS, 8, HALF), F32),
            vmem((2, LEVELS, 8, HALF // 2), F32),
            vmem((2, LEVELS, 8, HALF), F32),
            vmem((2, LEVELS, 8, HALF), F32),
            vmem((LEVELS, 8, HALF), F32),
            vmem((LEVELS, 8, HALF), F32),
            dma((5,)),
            dma((8,)), dma((8,)),
            dma((LEVELS,)), dma((LEVELS,)),
            dma((6, LEVELS)), dma((6, LEVELS)),
            dma((2, LEVELS)), dma((2, LEVELS)),
            dma((LEVELS,)), dma((LEVELS,)),
            dma((8, LEVELS)), dma((8, LEVELS)),
            dma((4, LEVELS)),
            dma((8, LEVELS)), dma((8, LEVELS)),
        ],
        compiler_params=pltpu.CompilerParams(collective_id=0, has_side_effects=True),
    )(increment, members, zonal_diff, merid_diff, sea_mask)


def solution(mesh):
    return jax.shard_map(
        shards,
        mesh=mesh,
        in_specs=(
            P(None, "gy", "gx"),
            P("mem", None, "gy", "gx"),
            P("gy", "gx"),
            P("gy", "gx"),
            P("gy", "gx"),
        ),
        out_specs=P(None, "gy", "gx"),
        check_vma=False,
    )
```
